32 devices in a mesh: groups: 2 (over y), blk: 4 (over z), split: 2 (over x), sub: 2 (over core).
Axes of the slice: x: 2, y: 2, z: 4, core: 2. Of those that a mesh axis runs over, the one named last changes fastest.
Arguments:
- attention_output_rows: bfloat16 [1024, 8192], P(('groups', 'blk'), 'split'), parts along dimension 0, may hold values from -6 to 6
- residual: bfloat16 [1024, 8192], P(('groups', 'split'), ('blk', 'sub')), parts along dimension 0, may hold values from -6 to 6
- output_projection_weight: bfloat16 [8192, 8192], P('split', ('blk', 'sub')), may hold values from -0.0625 to 0.0625
- down_adapter_bank: bfloat16 [4, 64, 8192], P('blk', None, 'split'), may hold values from -0.0625 to 0.0625
- up_adapter_bank: bfloat16 [4, 64, 8192], P('split', None, ('blk', 'sub')), may hold values from -0.75 to 0.75
- rollout_row_tenant: int32 [1024], P('groups'), parts along dimension 0, may hold values from 0 to 3, as said below
- tenant_bank_entry: int32 [4], replicated, may hold values from 0 to 3, each once
- tenant_live_rank: int32 [4], replicated, may hold values from 16 to 64, as said below
Outputs:
- layer_out: bfloat16 [1024, 8192], P(('groups', 'split'), ('blk', 'sub')), parts along dimension 0
The draws below stay inside these ranges and needn't reach their ends.
There are 2 independent parts, one for each index of `groups`. The reference program is written for one: setup_inputs(seed, part) draws one part's arguments, and reference() takes and returns one part's arrays. A program takes and returns all parts, laid end to end along the dimension named above; an argument that names none is the same for every part. Nothing has to cross between parts.
Inputs may be any that keep to these rules, and one draw needn't show every extreme that they name: `rollout_row_tenant`: every tenant owns at least one row of every part. `tenant_live_rank`: some tenant has the full rank 64.
All inputs are finite; a program needn't handle non-finite values.
Results may differ from the reference program's by a relative error of at most 0.0038.
Values may be sent and summed in bfloat16 or wider, within the bound.
A program may use at most 64 MiB of HBM per device.

```python
import jax
import jax.numpy as jnp

MODEL_WIDTH = 8192
PADDED_RANK = 64
TOKENS = 512
TENANT_TOTAL = 4


def draw_rollout_row_tenant(key, part):
    first_key, second_key, order_key, mix_key = jax.random.split(jax.random.fold_in(key, 11), 4)
    first = jax.random.randint(first_key, (TOKENS,), 0, TENANT_TOTAL)
    second = jax.random.randint(second_key, (TOKENS,), 0, TENANT_TOTAL)
    skewed = jnp.minimum(first, second)
    order = jax.random.permutation(order_key, TENANT_TOTAL)
    tenant_ids = order[skewed].astype(jnp.int32)
    tenant_ids = tenant_ids.at[:TENANT_TOTAL].set(jnp.arange(TENANT_TOTAL, dtype=jnp.int32))
    return jax.random.permutation(mix_key, tenant_ids).astype(jnp.int32)


def draw_tenant_live_rank(key, part):
    value_key, place_key = jax.random.split(jax.random.fold_in(key, 23), 2)
    ranks = jax.random.randint(value_key, (TENANT_TOTAL,), PADDED_RANK // 4, PADDED_RANK + 1)
    position = jax.random.randint(place_key, (), 0, TENANT_TOTAL)
    return ranks.at[position].set(PADDED_RANK).astype(jnp.int32)


def levels(own_key, extent, shards, smallest, largest):
    loudness = 1.0
    for dim, blocks in shards:
        heights = jax.random.uniform(jax.random.fold_in(jax.random.fold_in(own_key, 6), dim), (blocks,), jnp.float32, smallest / len(shards), largest / len(shards))
        loudness = loudness * jnp.repeat(jnp.exp(heights), extent[dim] // blocks).reshape((-1,) + (1,) * (len(extent) - 1 - dim))
    return loudness


def noise(key, dims, width, reach, pieces=(), held_as=jnp.bfloat16):
    values = width * jax.random.normal(key, dims, jnp.float32)
    if pieces:
        values = values * levels(key, dims, pieces, -0.22, 0.18)
    return jnp.clip(values, -reach, reach).astype(held_as)


def setup_inputs(seed: int = 0, part: int = 0) -> dict:
    keys = jax.random.split(jax.random.key(seed), 9)
    part_keys = jax.random.split(jax.random.fold_in(keys[8], part), 9)
    return {
        "attention_output_rows": noise(part_keys[0], (TOKENS, MODEL_WIDTH), 1.0, 6.0, ((0, 4), (1, 2))),
        "residual": noise(part_keys[1], (TOKENS, MODEL_WIDTH), 1.0, 6.0, ((0, 2), (1, 8))),
        "output_projection_weight": noise(keys[2], (MODEL_WIDTH, MODEL_WIDTH), MODEL_WIDTH ** -0.5, 0.0625, ((0, 2), (1, 8))),
        "down_adapter_bank": noise(keys[3], (TENANT_TOTAL, PADDED_RANK, MODEL_WIDTH), MODEL_WIDTH ** -0.5, 0.0625, ((0, 4), (2, 2))),
        "up_adapter_bank": noise(keys[4], (TENANT_TOTAL, PADDED_RANK, MODEL_WIDTH), PADDED_RANK ** -0.5, 0.75, ((0, 2), (2, 8))),
        "rollout_row_tenant": draw_rollout_row_tenant(jax.random.fold_in(jax.random.fold_in(keys[8], part), 71), part),
        "tenant_bank_entry": jax.random.permutation(keys[6], TENANT_TOTAL).astype(jnp.int32),
        "tenant_live_rank": draw_tenant_live_rank(jax.random.fold_in(keys[8], 71), part),
    }


def reference(attention_output_rows, residual, output_projection_weight, down_adapter_bank, up_adapter_bank, rollout_row_tenant, tenant_bank_entry, tenant_live_rank):
    frozen_output_term = jnp.dot(attention_output_rows, output_projection_weight, preferred_element_type=jnp.float32)
    slot_row = tenant_bank_entry[rollout_row_tenant]
    rank_row = tenant_live_rank[rollout_row_tenant]
    reduced_rank_rows = jnp.dot(attention_output_rows, down_adapter_bank.reshape(TENANT_TOTAL * PADDED_RANK, MODEL_WIDTH).T, preferred_element_type=jnp.float32)
    low_rank = jnp.take_along_axis(reduced_rank_rows.reshape(TOKENS, TENANT_TOTAL, PADDED_RANK), slot_row[:, None, None], axis=1)[:, 0, :]
    kept_mask = jnp.arange(PADDED_RANK)[None, :] < rank_row[:, None]
    scaling = PADDED_RANK / rank_row.astype(jnp.float32)
    low_scaled = jnp.where(kept_mask, low_rank * scaling[:, None], 0.0).astype(jnp.bfloat16)
    slot_hot = slot_row[:, None] == jnp.arange(TENANT_TOTAL)[None, :]
    rank_expanded_rows = jnp.where(slot_hot[:, :, None], low_scaled[:, None, :], jnp.zeros((), jnp.bfloat16)).reshape(TOKENS, TENANT_TOTAL * PADDED_RANK)
    adapter_output_term = jnp.dot(rank_expanded_rows, up_adapter_bank.reshape(TENANT_TOTAL * PADDED_RANK, MODEL_WIDTH), preferred_element_type=jnp.float32)
    return (residual.astype(jnp.float32) + frozen_output_term + adapter_output_term).astype(jnp.bfloat16)
```

```python
import functools

import jax
import jax.numpy as jnp
from jax import lax
from jax.experimental import pallas as pl
from jax.experimental.pallas import tpu as pltpu
from jax.sharding import PartitionSpec as P

PIECE = 256
FLIGHT = 2
LEAD = FLIGHT + 1
W_CHUNKS = 8
MESH = pl.DeviceIdType.MESH
F32 = jnp.float32


def kernel(
    nb, ns, nu, fc,
    ent_ref, rank_ref, x_ref, r_ref, w_ref, dn_ref, up_ref, ten_ref, o_ref,
    xown, xall, wv, rv, dnp, upp, mtab, acc, xs, xr, lacc, ls, lr, lowx,
    sem_loc, sem_w, sem_bank, sem_up, ready, zsend, zrecv, csend, crecv,
    usend, urecv, bsend, brecv, psend, precv, lsend, lrecv, gsend, grecv, fsend, frecv,
):
    blk, split, sub = lax.axis_index("blk"), lax.axis_index("split"), lax.axis_index("sub")
    rows, feats = x_ref.shape
    cols = w_ref.shape[1]
    own = r_ref.shape[0]
    banks, rank = dn_ref.shape[0], dn_ref.shape[1]
    up_banks = up_ref.shape[0]
    wide = dnp.shape[0]
    total = ten_ref.shape[1]
    tenants = ent_ref.shape[0]
    per = own // rows
    half = feats // nu
    pieces = half // fc
    share = rows // nu
    group = nb // 2
    upper = blk // group
    middle = group - 1 + upper
    in_middle = blk == middle
    ticks = (nb - 1) * pieces

    x_load = pltpu.make_async_copy(x_ref, xown, sem_loc.at[0])
    x_load.start()
    wrows = feats // W_CHUNKS
    w_loads = [
        pltpu.make_async_copy(
            w_ref.at[pl.ds(n * wrows, wrows)], wv.at[pl.ds(n * wrows, wrows)], sem_w.at[n]
        )
        for n in range(W_CHUNKS)
    ]
    for load in w_loads:
        load.start()

    barrier = pltpu.get_barrier_semaphore()

    @pl.when(blk < nb - 1)
    def _():
        pl.semaphore_signal(barrier, inc=1, device_id={"blk": blk + 1}, device_id_type=MESH)

    for k in range(1, ns):
        pl.semaphore_signal(
            barrier, inc=1, device_id={"split": lax.rem(split + k, ns)}, device_id_type=MESH
        )
    for k in range(1, nu):
        pl.semaphore_signal(
            barrier, inc=1, device_id={"sub": lax.rem(sub + k, nu)}, device_id_type=MESH
        )
    pl.semaphore_wait(barrier, ns + nu - 2 + jnp.where(blk > 0, 1, 0))

    def arrivals(side):
        return (nb - 1 - blk if side == 0 else blk) * pieces

    def sends(side):
        if side == 0:
            return jnp.where(blk > 0, nb - blk, 0) * pieces
        return jnp.where(blk < nb - 1, blk + 1, 0) * pieces

    def order(side, to, i):
        sign = 1 - 2 * side
        near = to + sign
        end = 0 if side == 0 else nb - 1
        late = (to == end) & (jnp.clip(near, 0, nb - 1) // per == split)
        body = (nb - 2) * pieces
        first = i < LEAD
        last = i >= LEAD + body
        j = i - LEAD
        b_late = jnp.where(first | last, near, near + sign * (1 + j // pieces))
        q_late = jnp.where(first, i, jnp.where(last, i - body, lax.rem(j + pieces, pieces)))
        b = jnp.where(late, b_late, near + sign * (i // pieces))
        q = jnp.where(late, q_late, lax.rem(i, pieces))
        return jnp.clip(b, 0, nb - 1), jnp.clip(q, 0, pieces - 1)

    def z_copy(side, i, to, mine=False):
        b, q = order(side, to, i)
        dst = xall.at[b, sub, q]
        src = dst
        if mine:
            src = x_ref.at[:, pl.ds(pl.multiple_of(sub * half + q * fc, fc), fc)]
        return pltpu.make_async_remote_copy(
            src_ref=src,
            dst_ref=dst,
            send_sem=zsend.at[side, i],
            recv_sem=zrecv.at[side, i],
            device_id={"blk": jnp.where(to == blk, lax.rem(blk + 1, nb), jnp.clip(to, 0, nb - 1))},
            device_id_type=MESH,
        )

    def target(side):
        return blk - 1 if side == 0 else blk + 1

    def send(side, i):
        to = target(side)
        b, _ = order(side, to, i)

        @pl.when((i < sends(side)) & (b == blk))
        def _():
            z_copy(side, i, to, True).start()

        @pl.when((i < sends(side)) & (b != blk))
        def _():
            z_copy(side, i, to).start()

    def c_copy(side, i, k, core):
        b, q = order(side, blk, i)
        piece = xall.at[b, core, q]
        return pltpu.make_async_remote_copy(
            src_ref=piece,
            dst_ref=piece,
            send_sem=csend.at[k - 1, side, i],
            recv_sem=crecv.at[k - 1, side, i],
            device_id={"sub": lax.rem(sub + k, nu)},
            device_id_type=MESH,
        )

    for i in range(FLIGHT):
        send(0, i)

    @pl.when(blk > 0)
    def _():
        pl.semaphore_signal(ready, inc=1, device_id={"blk": blk - 1}, device_id_type=MESH)

    @pl.when(blk < nb - 1)
    def _():
        pl.semaphore_wait(ready, 1)

    for i in range(FLIGHT):
        send(1, i)

    r_load = pltpu.make_async_copy(r_ref, rv, sem_loc.at[1])
    r_load.start()

    def bank_slot(place, e):
        return dnp.at[pl.ds(pl.multiple_of((place * banks + e) * rank, rank), rank)]

    bank_loads = [
        pltpu.make_async_copy(dn_ref.at[e], bank_slot(blk % group, e), sem_bank.at[e])
        for e in range(banks)
    ]

    @pl.when(in_middle)
    def _():
        for load in bank_loads:
            load.start()

    def up_slot(bank):
        return upp.at[pl.ds(pl.multiple_of(bank * rank, rank), rank)]

    up_loads = [
        pltpu.make_async_copy(up_ref.at[e], up_slot(split * up_banks + e), sem_up.at[e])
        for e in range(up_banks)
    ]
    for load in up_loads:
        load.start()

    def u_copy(k, e, owner):
        return pltpu.make_async_remote_copy(
            src_ref=up_ref.at[e],
            dst_ref=up_slot(owner * up_banks + e),
            send_sem=usend.at[k - 1, e],
            recv_sem=urecv.at[k - 1, e],
            device_id={"split": lax.rem(split + k, ns)},
            device_id_type=MESH,
        )

    for k in range(1, ns):
        for e in range(up_banks):
            u_copy(k, e, split).start()

    def b_copy(e, place):
        return pltpu.make_async_remote_copy(
            src_ref=dn_ref.at[e],
            dst_ref=bank_slot(place, e),
            send_sem=bsend.at[e],
            recv_sem=brecv.at[place, e],
            device_id={"blk": middle},
            device_id_type=MESH,
        )

    def p_copy(b, src):
        owner = b // per
        return pltpu.make_async_remote_copy(
            src_ref=xs.at[b],
            dst_ref=xr.at[src, b - owner * per],
            send_sem=psend.at[b],
            recv_sem=precv.at[src, b - owner * per],
            device_id={"split": owner},
            device_id_type=MESH,
        )

    def l_copy(b, src):
        owner = b // per
        return pltpu.make_async_remote_copy(
            src_ref=ls.at[b],
            dst_ref=lr.at[src, b - owner * per],
            send_sem=lsend.at[b],
            recv_sem=lrecv.at[src, b - owner * per],
            device_id={"split": owner},
            device_id_type=MESH,
        )

    def g_copy(k, h):
        return pltpu.make_async_remote_copy(
            src_ref=lowx.at[h, sub],
            dst_ref=lowx.at[h, sub],
            send_sem=gsend.at[k - 1],
            recv_sem=grecv.at[h],
            device_id={"blk": lax.rem(blk + k, nb)},
            device_id_type=MESH,
        )

    def f_copy(k, h, core):
        return pltpu.make_async_remote_copy(
            src_ref=lowx.at[h, core],
            dst_ref=lowx.at[h, core],
            send_sem=fsend.at[k - 1, h],
            recv_sem=frecv.at[k - 1, h],
            device_id={"sub": lax.rem(sub + k, nu)},
            device_id_type=MESH,
        )

    @pl.when(in_middle)
    def _():
        lane = lax.broadcasted_iota(jnp.int32, (1, wide), 1)
        tcol = jnp.transpose(jnp.broadcast_to(ten_ref[...].astype(F32), (8, total)))[:, :1]
        table = jnp.zeros((total, wide), F32)
        for t in range(tenants):
            live = jnp.full((1, wide), rank_ref[t], jnp.int32)
            slot = jnp.full((1, wide), ent_ref[t], jnp.int32)
            line = jnp.zeros((1, wide), F32)
            for e in range(group * banks):
                keep = (
                    (lane >= e * rank) & (lane < e * rank + jnp.minimum(live, rank))
                    & (slot == upper * group * banks + e)
                )
                line = jnp.where(keep, rank / live.astype(F32), line)
            table = jnp.where(tcol == t, line, table)
        mtab[...] = table

    def finish(b):
        @pl.when(b // per != split)
        def _():
            xs[b] = acc[b].astype(xs.dtype)
            p_copy(b, split).start()

    x_load.wait()
    for n, load in enumerate(w_loads):
        load.wait()
        here = slice(n * wrows, (n + 1) * wrows)
        part = jnp.dot(xown[:, here], wv[here, :], preferred_element_type=F32)
        if n == 0:
            acc[blk] = part
        else:
            acc[blk] += part
    finish(blk)

    def compute(side, i):
        @pl.when((i >= 0) & (i < arrivals(side)))
        def _():
            b, q = order(side, blk, i)
            for k in range(1, nu):
                c_copy(side, i, k, lax.rem(sub - k + nu, nu)).wait_recv()
            part = jnp.zeros((rows, cols), F32)
            for c in range(nu):
                at = pl.ds(pl.multiple_of(c * half + q * fc, fc), fc)
                part = part + jnp.dot(xall[b, c, q], wv[at, :], preferred_element_type=F32)

            @pl.when(q == 0)
            def _():
                acc[b] = part

            @pl.when(q != 0)
            def _():
                acc[b] += part

            for k in range(1, nu):
                c_copy(side, i, k, sub).wait_send()

            @pl.when(q == pieces - 1)
            def _():
                finish(b)

    def low_work():
        for load in bank_loads:
            load.wait()
        for p in range(group):
            @pl.when(p != blk % group)
            def _():
                for e in range(banks):
                    b_copy(e, p).wait_recv()

        part_rows = pl.ds(pl.multiple_of(sub * share, share), share)

        def put(b, low):
            @pl.when(b // per == split)
            def _():
                lacc[b - split * per] = low

            @pl.when(b // per != split)
            def _():
                ls[b] = low
                l_copy(b, split).start()

        put(blk, lax.dot_general(
            xown[part_rows, :], dnp[...], (((1,), (1,)), ((), ())), preferred_element_type=F32
        ))

        @pl.loop(1, nb)
        def _(n):
            b = lax.rem(blk + n, nb)
            x = jnp.concatenate(
                [xall[b, c, q, part_rows, :] for c in range(nu) for q in range(pieces)], axis=1
            )
            put(b, lax.dot_general(
                x, dnp[...], (((1,), (1,)), ((), ())), preferred_element_type=F32
            ))

    def low_spread():
        for o in range(per):
            b = split * per + o
            low = lacc[o]
            for k in range(1, ns):
                src = lax.rem(split + k, ns)
                l_copy(b, src).wait_recv()
                low = low + lr[src, o]
            scale = mtab[pl.ds(pl.multiple_of(b * rows + sub * share, share), share), :]
            lowx[upper, sub, o] = (low * scale).astype(lowx.dtype)
        for k in range(1, nb):
            g_copy(k, upper).start()

    def low_share():
        for h in range(2):
            @pl.when(jnp.logical_not(in_middle & (upper == h)))
            def _():
                g_copy(1, h).wait_recv()
            for k in range(1, nu):
                f_copy(k, h, sub).start()

    low_tick = group * pieces + 1
    away = jnp.where(upper == 0, middle - blk, blk - middle)
    bank_tick = jnp.maximum(pieces, (away - 1) * pieces + 1)

    @pl.loop(0, ticks + 1)
    def _(t):
        for side in range(2):
            @pl.when((t >= 1) & (t - 1 < arrivals(side)))
            def _():
                z_copy(side, t - 1, blk).wait_recv()
                for k in range(1, nu):
                    c_copy(side, t - 1, k, sub).start()

            @pl.when((t < ticks) & (t + FLIGHT < sends(side)))
            def _():
                z_copy(side, t, target(side)).wait_send()
                send(side, t + FLIGHT)

        @pl.when((t == bank_tick) & jnp.logical_not(in_middle))
        def _():
            for e in range(banks):
                b_copy(e, blk % group).start()

        @pl.when(t == ticks - 1)
        def _():
            low_share()

        for side in range(2):
            compute(side, t - 2)

        @pl.when((t == low_tick) & in_middle)
        def _():
            low_work()

        @pl.when((t == low_tick + 2) & in_middle)
        def _():
            low_spread()

    r_load.wait()
    for load in up_loads:
        load.wait()
    for k in range(1, ns):
        for e in range(up_banks):
            u_copy(k, e, lax.rem(split - k + ns, ns)).wait_recv()
    for h in range(2):
        for k in range(1, nu):
            f_copy(k, h, lax.rem(sub - k + nu, nu)).wait_recv()

    for o in range(per):
        b = split * per + o
        here = slice(o * rows, (o + 1) * rows)
        low = jnp.concatenate(
            [
                jnp.concatenate([lowx[h, c, o] for h in range(2)], axis=1)
                for c in range(nu)
            ],
            axis=0,
        )
        value = acc[b] + rv[here, :].astype(F32)
        value = value + jnp.dot(low, upp[...], preferred_element_type=F32)
        for k in range(1, ns):
            src = lax.rem(split + k, ns)
            p_copy(b, src).wait_recv()
            value = value + xr[src, o].astype(F32)
        acc[b] = value

    for side in range(2):
        compute(side, ticks - 1)

    for o in range(per):
        here = slice(o * rows, (o + 1) * rows)
        o_ref[here, :] = acc[split * per + o].astype(o_ref.dtype)

    for side in range(2):
        for n in range(FLIGHT):
            @pl.when(sends(side) > 0)
            def _():
                z_copy(side, sends(side) - FLIGHT + n, target(side)).wait_send()
    for k in range(1, ns):
        for e in range(up_banks):
            u_copy(k, e, split).wait_send()

    @pl.when(jnp.logical_not(in_middle))
    def _():
        for e in range(banks):
            b_copy(e, blk % group).wait_send()

    for b in range(nb):
        @pl.when(b // per != split)
        def _():
            p_copy(b, split).wait_send()

            @pl.when(in_middle)
            def _():
                l_copy(b, split).wait_send()

    @pl.when(in_middle)
    def _():
        for k in range(1, nb):
            g_copy(k, upper).wait_send()

    for h in range(2):
        for k in range(1, nu):
            f_copy(k, h, sub).wait_send()


def shards(
    nb, ns, nu,
    attention_output_rows,
    residual,
    output_projection_weight,
    down_adapter_bank,
    up_adapter_bank,
    rollout_row_tenant,
    tenant_bank_entry,
    tenant_live_rank,
):
    rows, feats = attention_output_rows.shape
    own, cols = residual.shape
    banks, rank, _ = down_adapter_bank.shape
    up_banks = up_adapter_bank.shape[0]
    total = rollout_row_tenant.shape[0]
    wide = nb // 2 * banks * rank
    fc = PIECE
    per = own // rows
    pieces = feats // nu // fc
    items = (nb - 1) * pieces
    share = rows // nu
    dma = pltpu.SemaphoreType.DMA
    bf16 = jnp.bfloat16
    any_spec = pl.BlockSpec(memory_space=pl.ANY)
    smem = pl.BlockSpec(memory_space=pltpu.SMEM)
    vmem = pl.BlockSpec(memory_space=pltpu.VMEM)
    return pl.pallas_call(
        functools.partial(kernel, nb, ns, nu, fc),
        out_shape=jax.ShapeDtypeStruct((own, cols), bf16),
        in_specs=[smem, smem] + [any_spec] * 5 + [vmem],
        out_specs=vmem,
        scratch_shapes=[
            pltpu.VMEM((rows, feats), bf16),
            pltpu.VMEM((nb, nu, pieces, rows, fc), bf16),
            pltpu.VMEM((feats, cols), bf16),
            pltpu.VMEM((own, cols), bf16),
            pltpu.VMEM((wide, feats), bf16),
            pltpu.VMEM((2 * wide, cols), bf16),
            pltpu.VMEM((total, wide), F32),
            pltpu.VMEM((nb, rows, cols), F32),
            pltpu.VMEM((nb, rows, cols), bf16),
            pltpu.VMEM((ns, per, rows, cols), bf16),
            pltpu.VMEM((per, share, wide), F32),
            pltpu.VMEM((nb, share, wide), F32),
            pltpu.VMEM((ns, per, share, wide), F32),
            pltpu.VMEM((2, nu, per, share, wide), bf16),
            dma((2,)),
            dma((W_CHUNKS,)),
            dma((banks,)),
            dma((up_banks,)),
            pltpu.SemaphoreType.REGULAR,
            dma((2, nb * pieces)),
            dma((2, nb * pieces)),
            dma((nu - 1, 2, items)),
            dma((nu - 1, 2, items)),
            dma((ns - 1, up_banks)),
            dma((ns - 1, up_banks)),
            dma((banks,)),
            dma((nb // 2, banks)),
            dma((nb,)),
            dma((ns, per)),
            dma((nb,)),
            dma((ns, per)),
            dma((nb - 1,)),
            dma((2,)),
            dma((nu - 1, 2)),
            dma((nu - 1, 2)),
        ],
        compiler_params=pltpu.CompilerParams(
            collective_id=0, has_side_effects=True, vmem_limit_bytes=44 * 2**20
        ),
    )(
        tenant_bank_entry,
        tenant_live_rank,
        attention_output_rows,
        residual,
        output_projection_weight,
        down_adapter_bank,
        up_adapter_bank,
        rollout_row_tenant.reshape(1, total),
    )


def solution(mesh):
    in_specs = (
        P(("groups", "blk"), "split"),
        P(("groups", "split"), ("blk", "sub")),
        P("split", ("blk", "sub")),
        P("blk", None, "split"),
        P("split", None, ("blk", "sub")),
        P("groups"),
        P(),
        P(),
    )
    out_specs = P(("groups", "split"), ("blk", "sub"))
    body = functools.partial(
        shards, mesh.shape["blk"], mesh.shape["split"], mesh.shape["sub"]
    )
    return jax.shard_map(body, mesh=mesh, in_specs=in_specs, out_specs=out_specs, check_vma=False)
```

```python
import functools

import jax
import jax.numpy as jnp
from jax import lax
from jax.experimental import pallas as pl
from jax.experimental.pallas import tpu as pltpu
from jax.sharding import PartitionSpec as P

PIECE = 256
FLIGHT = 3
LEAD = FLIGHT + 1
W_CHUNKS = 4
LOW_BLOCKS = 4
MESH = pl.DeviceIdType.MESH
F32 = jnp.float32


def kernel(
    nb, ns, nu, fc,
    ent_any, rank_any, x_ref, r_ref, w_ref, dn_ref, up_ref, ten_any, o_ref,
    ent_ref, rank_ref, ten_ref, xown, xall, wv, rv, dnp, upp, mtab, acc, xs, xr, lacc, ls, lr, lowx,
    sem_loc, sem_w, sem_bank, sem_up, ready, zsend, zrecv, csend, crecv,
    usend, urecv, bsend, brecv, psend, precv, lsend, lrecv, gsend, grecv, fsend, frecv,
):
    blk, split, sub = lax.axis_index("blk"), lax.axis_index("split"), lax.axis_index("sub")
    rows, feats = x_ref.shape
    cols = w_ref.shape[1]
    own = r_ref.shape[0]
    banks, rank = dn_ref.shape[0], dn_ref.shape[1]
    up_banks = up_ref.shape[0]
    wide = dnp.shape[0]
    total = ten_ref.shape[1]
    tenants = ent_ref.shape[0]
    per = own // rows
    half = feats // nu
    pieces = half // fc
    share = rows // nu
    group = nb // 2
    upper = blk // group
    middle = group - 1 + upper
    in_middle = blk == middle
    ticks = (nb - 1) * pieces

    x_load = pltpu.make_async_copy(x_ref, xown, sem_loc.at[0])
    x_load.start()
    wrows = feats // W_CHUNKS
    w_loads = [
        pltpu.make_async_copy(
            w_ref.at[pl.ds(n * wrows, wrows)], wv.at[pl.ds(n * wrows, wrows)], sem_w.at[n]
        )
        for n in range(W_CHUNKS)
    ]
    for load in w_loads:
        load.start()

    barrier = pltpu.get_barrier_semaphore()

    @pl.when(blk < nb - 1)
    def _():
        pl.semaphore_signal(barrier, inc=1, device_id={"blk": blk + 1}, device_id_type=MESH)

    for k in range(1, ns):
        pl.semaphore_signal(
            barrier, inc=1, device_id={"split": lax.rem(split + k, ns)}, device_id_type=MESH
        )
    for k in range(1, nu):
        pl.semaphore_signal(
            barrier, inc=1, device_id={"sub": lax.rem(sub + k, nu)}, device_id_type=MESH
        )
    pl.semaphore_wait(barrier, ns + nu - 2 + jnp.where(blk > 0, 1, 0))

    def arrivals(side):
        return (nb - 1 - blk if side == 0 else blk) * pieces

    def sends(side):
        if side == 0:
            return jnp.where(blk > 0, nb - blk, 0) * pieces
        return jnp.where(blk < nb - 1, blk + 1, 0) * pieces

    def order(side, to, i):
        sign = 1 - 2 * side
        near = to + sign
        end = 0 if side == 0 else nb - 1
        late = (to == end) & (jnp.clip(near, 0, nb - 1) // per == split)
        body = (nb - 2) * pieces
        first = i < LEAD
        last = i >= LEAD + body
        j = i - LEAD
        b_late = jnp.where(first | last, near, near + sign * (1 + j // pieces))
        q_late = jnp.where(first, i, jnp.where(last, i - body, lax.rem(j + pieces, pieces)))
        b = jnp.where(late, b_late, near + sign * (i // pieces))
        q = jnp.where(late, q_late, lax.rem(i, pieces))
        return jnp.clip(b, 0, nb - 1), jnp.clip(q, 0, pieces - 1)

    def z_copy(side, i, to, mine=False):
        b, q = order(side, to, i)
        dst = xall.at[b, sub, q]
        src = dst
        if mine:
            src = x_ref.at[:, pl.ds(pl.multiple_of(sub * half + q * fc, fc), fc)]
        return pltpu.make_async_remote_copy(
            src_ref=src,
            dst_ref=dst,
            send_sem=zsend.at[side, lax.rem(i, FLIGHT)],
            recv_sem=zrecv.at[i if side == 0 else ticks - 1 - i],
            device_id={"blk": jnp.where(to == blk, lax.rem(blk + 1, nb), jnp.clip(to, 0, nb - 1))},
            device_id_type=MESH,
        )

    def target(side):
        return blk - 1 if side == 0 else blk + 1

    def send(side, i):
        to = target(side)
        b, _ = order(side, to, i)

        @pl.when((i < sends(side)) & (b == blk))
        def _():
            z_copy(side, i, to, True).start()

        @pl.when((i < sends(side)) & (b != blk))
        def _():
            z_copy(side, i, to).start()

    def c_copy(side, i, k, core):
        b, q = order(side, blk, i)
        piece = xall.at[b, core, q]
        return pltpu.make_async_remote_copy(
            src_ref=piece,
            dst_ref=piece,
            send_sem=csend.at[k - 1, side, lax.rem(i, 2)],
            recv_sem=crecv.at[k - 1, i if side == 0 else ticks - 1 - i],
            device_id={"sub": lax.rem(sub + k, nu)},
            device_id_type=MESH,
        )

    @pl.when(blk > 0)
    def _():
        pl.semaphore_signal(ready, inc=1, device_id={"blk": blk - 1}, device_id_type=MESH)

    for i in range(FLIGHT):
        send(0, i)

    @pl.when(blk < nb - 1)
    def _():
        pl.semaphore_wait(ready, 1)

    for i in range(FLIGHT):
        send(1, i)

    r_load = pltpu.make_async_copy(r_ref, rv, sem_loc.at[1])
    r_load.start()

    def bank_slot(place, e):
        return dnp.at[pl.ds(pl.multiple_of((place * banks + e) * rank, rank), rank)]

    table_loads = [
        pltpu.make_async_copy(src, dst, sem_loc.at[2 + n])
        for n, (src, dst) in enumerate(
            ((ent_any, ent_ref), (rank_any, rank_ref), (ten_any, ten_ref))
        )
    ]
    bank_loads = [
        pltpu.make_async_copy(dn_ref.at[e], bank_slot(blk % group, e), sem_bank.at[e])
        for e in range(banks)
    ]

    @pl.when(in_middle)
    def _():
        for load in table_loads + bank_loads:
            load.start()

    def up_slot(bank):
        return upp.at[pl.ds(pl.multiple_of(bank * rank, rank), rank)]

    up_loads = [
        pltpu.make_async_copy(up_ref.at[e], up_slot(split * up_banks + e), sem_up.at[e])
        for e in range(up_banks)
    ]
    for load in up_loads:
        load.start()

    def u_copy(k, e, owner):
        return pltpu.make_async_remote_copy(
            src_ref=up_ref.at[e],
            dst_ref=up_slot(owner * up_banks + e),
            send_sem=usend.at[k - 1, e],
            recv_sem=urecv.at[k - 1, e],
            device_id={"split": lax.rem(split + k, ns)},
            device_id_type=MESH,
        )

    for k in range(1, ns):
        for e in range(up_banks):
            u_copy(k, e, split).start()

    def b_copy(e, place):
        return pltpu.make_async_remote_copy(
            src_ref=dn_ref.at[e],
            dst_ref=bank_slot(place, e),
            send_sem=bsend.at[e],
            recv_sem=brecv.at[place, e],
            device_id={"blk": middle},
            device_id_type=MESH,
        )

    def p_copy(b, src):
        owner = b // per
        return pltpu.make_async_remote_copy(
            src_ref=xs.at[b],
            dst_ref=xr.at[src, b - owner * per],
            send_sem=psend.at[b],
            recv_sem=precv.at[src, b - owner * per],
            device_id={"split": owner},
            device_id_type=MESH,
        )

    def l_copy(b, src):
        owner = b // per
        return pltpu.make_async_remote_copy(
            src_ref=ls.at[b],
            dst_ref=lr.at[src, b - owner * per],
            send_sem=lsend.at[b],
            recv_sem=lrecv.at[src, b - owner * per],
            device_id={"split": owner},
            device_id_type=MESH,
        )

    def g_copy(k, h):
        return pltpu.make_async_remote_copy(
            src_ref=lowx.at[h, sub],
            dst_ref=lowx.at[h, sub],
            send_sem=gsend.at[k - 1],
            recv_sem=grecv.at[h],
            device_id={"blk": lax.rem(blk + k, nb)},
            device_id_type=MESH,
        )

    def f_copy(k, h, core):
        return pltpu.make_async_remote_copy(
            src_ref=lowx.at[h, core],
            dst_ref=lowx.at[h, core],
            send_sem=fsend.at[k - 1, h],
            recv_sem=frecv.at[k - 1, h],
            device_id={"sub": lax.rem(sub + k, nu)},
            device_id_type=MESH,
        )

    @pl.when(in_middle)
    def _():
        for load in table_loads:
            load.wait()
        lane = lax.broadcasted_iota(jnp.int32, (1, wide), 1)
        tcol = jnp.transpose(jnp.broadcast_to(ten_ref[...].astype(F32), (8, total)))[:, :1]
        table = jnp.zeros((total, wide), F32)
        for t in range(tenants):
            live = jnp.full((1, wide), rank_ref[t], jnp.int32)
            slot = jnp.full((1, wide), ent_ref[t], jnp.int32)
            line = jnp.zeros((1, wide), F32)
            for e in range(group * banks):
                keep = (
                    (lane >= e * rank) & (lane < e * rank + jnp.minimum(live, rank))
                    & (slot == upper * group * banks + e)
                )
                line = jnp.where(keep, rank / live.astype(F32), line)
            table = jnp.where(tcol == t, line, table)
        mtab[...] = table

    def finish(b):
        @pl.when(b // per != split)
        def _():
            xs[b] = acc[b].astype(xs.dtype)
            p_copy(b, split).start()

    x_load.wait()

    @pl.when(in_middle)
    def _():
        for c in range(nu):
            for q in range(pieces):
                xall[blk, c, q] = xown[:, c * half + q * fc:c * half + (q + 1) * fc]

    for n, load in enumerate(w_loads):
        load.wait()
        here = slice(n * wrows, (n + 1) * wrows)
        part = jnp.dot(xown[:, here], wv[here, :], preferred_element_type=F32)
        if n == 0:
            acc[blk] = part
        else:
            acc[blk] += part
    finish(blk)

    def gather(side, i):
        @pl.when((i >= 0) & (i < arrivals(side)))
        def _():
            for k in range(1, nu):
                c_copy(side, i, k, lax.rem(sub - k + nu, nu)).wait_recv()
                c_copy(side, i, k, sub).wait_send()

    def compute(side, i):
        @pl.when((i >= 0) & (i < arrivals(side)))
        def _():
            b, q = order(side, blk, i)
            part = jnp.zeros((rows, cols), F32)
            for c in range(nu):
                at = pl.ds(pl.multiple_of(c * half + q * fc, fc), fc)
                part = part + jnp.dot(xall[b, c, q], wv[at, :], preferred_element_type=F32)

            @pl.when(q == 0)
            def _():
                acc[b] = part

            @pl.when(q != 0)
            def _():
                acc[b] += part

            @pl.when(q == pieces - 1)
            def _():
                finish(b)

    def low_work():
        for load in bank_loads:
            load.wait()
        for p in range(group):
            @pl.when(p != blk % group)
            def _():
                for e in range(banks):
                    b_copy(e, p).wait_recv()

        part_rows = pl.ds(pl.multiple_of(sub * share, share), share)

        def put(b, low):
            @pl.when(b // per == split)
            def _():
                lacc[b - split * per] = low

            @pl.when(b // per != split)
            def _():
                ls[b] = low
                l_copy(b, split).start()

        @pl.loop(0, nb // LOW_BLOCKS)
        def _(n):
            blocks = [lax.rem(blk + n * LOW_BLOCKS + m, nb) for m in range(LOW_BLOCKS)]
            low = jnp.zeros((LOW_BLOCKS * share, wide), F32)
            for c in range(nu):
                for q in range(pieces):
                    x = jnp.concatenate([xall[b, c, q, part_rows, :] for b in blocks], axis=0)
                    d = dnp[:, c * half + q * fc:c * half + (q + 1) * fc]
                    low = low + lax.dot_general(
                        x, d, (((1,), (1,)), ((), ())), preferred_element_type=F32
                    )
            for m, b in enumerate(blocks):
                put(b, low[m * share:(m + 1) * share])

    def low_spread():
        for o in range(per):
            b = split * per + o
            low = lacc[o]
            for k in range(1, ns):
                src = lax.rem(split + k, ns)
                l_copy(b, src).wait_recv()
                low = low + lr[src, o]
            scale = mtab[pl.ds(pl.multiple_of(b * rows + sub * share, share), share), :]
            lowx[upper, sub, o] = (low * scale).astype(lowx.dtype)
        for k in range(1, nb):
            g_copy(k, upper).start()

    def low_share():
        for h in range(2):
            @pl.when(jnp.logical_not(in_middle & (upper == h)))
            def _():
                g_copy(1, h).wait_recv()
            for k in range(1, nu):
                f_copy(k, h, sub).start()

    low_tick = group * pieces + 1
    away = jnp.where(upper == 0, middle - blk, blk - middle)
    bank_tick = jnp.maximum(pieces, (away - 1) * pieces + 1)

    @pl.loop(0, ticks + 1)
    def _(t):
        for side in range(2):
            @pl.when((t >= 1) & (t - 1 < arrivals(side)))
            def _():
                z_copy(side, t - 1, blk).wait_recv()
                for k in range(1, nu):
                    c_copy(side, t - 1, k, sub).start()

        @pl.when((t == low_tick + 1) & in_middle)
        def _():
            low_spread()

        for side in range(2):
            @pl.when((t < ticks) & (t + FLIGHT < sends(side)))
            def _():
                z_copy(side, t, target(side)).wait_send()
                send(side, t + FLIGHT)

        @pl.when((t == bank_tick) & jnp.logical_not(in_middle))
        def _():
            for e in range(banks):
                b_copy(e, blk % group).start()

        @pl.when(t == ticks)
        def _():
            low_share()

        for side in range(2):
            gather(side, t - 2)

        @pl.when((t == low_tick) & in_middle)
        def _():
            low_work()

        for side in range(2):
            compute(side, t - 2)

    r_load.wait()
    for load in up_loads:
        load.wait()
    for k in range(1, ns):
        for e in range(up_banks):
            u_copy(k, e, lax.rem(split - k + ns, ns)).wait_recv()
    for h in range(2):
        for k in range(1, nu):
            f_copy(k, h, lax.rem(sub - k + nu, nu)).wait_recv()

    for o in range(per):
        b = split * per + o
        here = slice(o * rows, (o + 1) * rows)
        low = jnp.concatenate(
            [
                jnp.concatenate([lowx[h, c, o] for h in range(2)], axis=1)
                for c in range(nu)
            ],
            axis=0,
        )
        value = acc[b] + rv[here, :].astype(F32)
        value = value + jnp.dot(low, upp[...], preferred_element_type=F32)
        for k in range(1, ns):
            src = lax.rem(split + k, ns)
            p_copy(b, src).wait_recv()
            value = value + xr[src, o].astype(F32)
        acc[b] = value

    for side in range(2):
        gather(side, ticks - 1)
        compute(side, ticks - 1)

    for o in range(per):
        here = slice(o * rows, (o + 1) * rows)
        o_ref[here, :] = acc[split * per + o].astype(o_ref.dtype)

    for side in range(2):
        for n in range(FLIGHT):
            @pl.when(sends(side) > 0)
            def _():
                z_copy(side, sends(side) - FLIGHT + n, target(side)).wait_send()
    for k in range(1, ns):
        for e in range(up_banks):
            u_copy(k, e, split).wait_send()

    @pl.when(jnp.logical_not(in_middle))
    def _():
        for e in range(banks):
            b_copy(e, blk % group).wait_send()

    for b in range(nb):
        @pl.when(b // per != split)
        def _():
            p_copy(b, split).wait_send()

            @pl.when(in_middle)
            def _():
                l_copy(b, split).wait_send()

    @pl.when(in_middle)
    def _():
        for k in range(1, nb):
            g_copy(k, upper).wait_send()

    for h in range(2):
        for k in range(1, nu):
            f_copy(k, h, sub).wait_send()


def shards(
    nb, ns, nu,
    attention_output_rows,
    residual,
    output_projection_weight,
    down_adapter_bank,
    up_adapter_bank,
    rollout_row_tenant,
    tenant_bank_entry,
    tenant_live_rank,
):
    rows, feats = attention_output_rows.shape
    own, cols = residual.shape
    banks, rank, _ = down_adapter_bank.shape
    up_banks = up_adapter_bank.shape[0]
    total = rollout_row_tenant.shape[0]
    wide = nb // 2 * banks * rank
    fc = PIECE
    per = own // rows
    pieces = feats // nu // fc
    items = (nb - 1) * pieces
    share = rows // nu
    dma = pltpu.SemaphoreType.DMA
    bf16 = jnp.bfloat16
    any_spec = pl.BlockSpec(memory_space=pltpu.HBM)
    vmem = pl.BlockSpec(memory_space=pltpu.VMEM)
    return pl.pallas_call(
        functools.partial(kernel, nb, ns, nu, fc),
        out_shape=pltpu.VMEM((own, cols), bf16),
        in_specs=[any_spec] * 8,
        out_specs=vmem,
        scratch_shapes=[
            pltpu.SMEM(tenant_bank_entry.shape, jnp.int32),
            pltpu.SMEM(tenant_live_rank.shape, jnp.int32),
            pltpu.VMEM((1, total), jnp.int32),
            pltpu.VMEM((rows, feats), bf16),
            pltpu.VMEM((nb, nu, pieces, rows, fc), bf16),
            pltpu.VMEM((feats, cols), bf16),
            pltpu.VMEM((own, cols), bf16),
            pltpu.VMEM((wide, feats), bf16),
            pltpu.VMEM((2 * wide, cols), bf16),
            pltpu.VMEM((total, wide), F32),
            pltpu.VMEM((nb, rows, cols), F32),
            pltpu.VMEM((nb, rows, cols), bf16),
            pltpu.VMEM((ns, per, rows, cols), bf16),
            pltpu.VMEM((per, share, wide), F32),
            pltpu.VMEM((nb, share, wide), F32),
            pltpu.VMEM((ns, per, share, wide), F32),
            pltpu.VMEM((2, nu, per, share, wide), bf16),
            dma((5,)),
            dma((W_CHUNKS,)),
            dma((banks,)),
            dma((up_banks,)),
            pltpu.SemaphoreType.REGULAR,
            dma((2, FLIGHT)),
            dma((items,)),
            dma((nu - 1, 2, 2)),
            dma((nu - 1, items)),
            dma((ns - 1, up_banks)),
            dma((ns - 1, up_banks)),
            dma((banks,)),
            dma((nb // 2, banks)),
            dma((nb,)),
            dma((ns, per)),
            dma((nb,)),
            dma((ns, per)),
            dma((nb - 1,)),
            dma((2,)),
            dma((nu - 1, 2)),
            dma((nu - 1, 2)),
        ],
        compiler_params=pltpu.CompilerParams(
            collective_id=0, has_side_effects=True, vmem_limit_bytes=60 * 2**20
        ),
    )(
        tenant_bank_entry,
        tenant_live_rank,
        attention_output_rows,
        residual,
        output_projection_weight,
        down_adapter_bank,
        up_adapter_bank,
        rollout_row_tenant.reshape(1, total),
    )


def solution(mesh):
    in_specs = (
        P(("groups", "blk"), "split"),
        P(("groups", "split"), ("blk", "sub")),
        P("split", ("blk", "sub")),
        P("blk", None, "split"),
        P("split", None, ("blk", "sub")),
        P("groups"),
        P(),
        P(),
    )
    out_specs = P(("groups", "split"), ("blk", "sub"))
    body = functools.partial(
        shards, mesh.shape["blk"], mesh.shape["split"], mesh.shape["sub"]
    )
    return jax.shard_map(body, mesh=mesh, in_specs=in_specs, out_specs=out_specs, check_vma=False)
```

```python
import functools

import jax
import jax.numpy as jnp
from jax import lax
from jax.experimental import pallas as pl
from jax.experimental.pallas import tpu as pltpu
from jax.sharding import PartitionSpec as P

PIECE = 256
FLIGHT = 4
LEAD = (4, 3)
W_CHUNKS = 4
EARLY = 2
MESH = pl.DeviceIdType.MESH
F32 = jnp.float32


def kernel(
    nb, ns, nu, fc,
    ent_any, rank_any, x_ref, r_ref, w_ref, dn_ref, up_ref, ten_any, o_ref,
    ent_ref, rank_ref, ten_ref, xown, xall, wv, rv, dnp, upp, mtab, acc, xs, xr, lacc, ls, lr, lowx, hot,
    sem_loc, sem_w, sem_bank, sem_up, ready, entered, zsend, zrecv, csend, crecv,
    usend, urecv, bsend, brecv, bcsend, bcrecv, psend, precv, lsend, lrecv, gsend, grecv, fsend, frecv,
):
    blk, split, sub = lax.axis_index("blk"), lax.axis_index("split"), lax.axis_index("sub")
    rows, feats = x_ref.shape
    cols = w_ref.shape[1]
    own = r_ref.shape[0]
    banks, rank = dn_ref.shape[0], dn_ref.shape[1]
    up_banks = up_ref.shape[0]
    wide = dnp.shape[0]
    total = ten_ref.shape[1]
    tenants = ent_ref.shape[0]
    per = own // rows
    half = feats // nu
    pieces = half // fc
    share = rows // nu
    group = nb // 2
    upper = blk // group
    middle = group - 1 + upper
    in_middle = blk == middle
    ticks = (nb - 1) * pieces

    barrier = pltpu.get_barrier_semaphore()

    @pl.when(blk < nb - 1)
    def _():
        pl.semaphore_signal(barrier, inc=1, device_id={"blk": blk + 1}, device_id_type=MESH)

    def peers(upper_ones, sem):
        for axis, n, me in (("split", ns, split), ("sub", nu, sub)):
            for k in range(1, n):
                to = me + k if upper_ones else me - k

                @pl.when(to < n if upper_ones else to >= 0)
                def _():
                    pl.semaphore_signal(
                        sem, inc=1, device_id={axis: jnp.clip(to, 0, n - 1)},
                        device_id_type=MESH,
                    )

    peers(True, barrier)
    below = jnp.where(blk > 0, 1, 0) + split + sub

    @pl.when(below > 0)
    def _():
        pl.semaphore_wait(barrier, below)


    def arrivals(side):
        return (nb - 1 - blk if side == 0 else blk) * pieces

    def sends(side):
        if side == 0:
            return jnp.where(blk > 0, nb - blk, 0) * pieces
        return jnp.where(blk < nb - 1, blk + 1, 0) * pieces

    def is_late(side, to):
        near = jnp.clip(to + 1 - 2 * side, 0, nb - 1)
        return (to == (0 if side == 0 else nb - 1)) & (near // per == split)

    def order(side, to, i):
        sign = 1 - 2 * side
        near = to + sign
        late = is_late(side, to)
        body = (nb - 2) * pieces
        lead = LEAD[side]
        first = i < lead
        last = i >= lead + body
        j = i - lead
        b_late = jnp.where(first | last, near, near + sign * (1 + j // pieces))
        q_late = jnp.where(first, i, jnp.where(last, i - body, lax.rem(j + pieces, pieces)))
        b = jnp.where(late, b_late, near + sign * (i // pieces))
        q = jnp.where(late, q_late, lax.rem(i, pieces))
        return jnp.clip(b, 0, nb - 1), jnp.clip(q, 0, pieces - 1)

    def z_copy(side, i, to, mine=False):
        b, q = order(side, to, i)
        dst = xall.at[b, sub, q]
        src = dst
        if mine:
            src = x_ref.at[:, pl.ds(pl.multiple_of(sub * half + q * fc, fc), fc)]
        return pltpu.make_async_remote_copy(
            src_ref=src,
            dst_ref=dst,
            send_sem=zsend.at[side, lax.rem(i, FLIGHT)],
            recv_sem=zrecv.at[i if side == 0 else ticks - 1 - i],
            device_id={"blk": jnp.where(to == blk, lax.rem(blk + 1, nb), jnp.clip(to, 0, nb - 1))},
            device_id_type=MESH,
        )

    def target(side):
        return blk - 1 if side == 0 else blk + 1

    def flight(side):
        return jnp.where(is_late(side, target(side)), LEAD[side] - 1, FLIGHT)

    def send(side, i):
        to = target(side)
        b, _ = order(side, to, i)

        @pl.when((i < sends(side)) & (b == blk))
        def _():
            z_copy(side, i, to, True).start()

        @pl.when((i < sends(side)) & (b != blk))
        def _():
            z_copy(side, i, to).start()

    def c_copy(side, i, k, core):
        b, q = order(side, blk, i)
        piece = xall.at[b, core, q]
        return pltpu.make_async_remote_copy(
            src_ref=piece,
            dst_ref=piece,
            send_sem=csend.at[k - 1, side, lax.rem(i, 2)],
            recv_sem=crecv.at[k - 1, i if side == 0 else ticks - 1 - i],
            device_id={"sub": lax.rem(sub + k, nu)},
            device_id_type=MESH,
        )

    x_load = pltpu.make_async_copy(x_ref, xown, sem_loc.at[0])
    wrows = feats // W_CHUNKS
    w_loads = [
        pltpu.make_async_copy(
            w_ref.at[pl.ds(n * wrows, wrows)], wv.at[pl.ds(n * wrows, wrows)], sem_w.at[n]
        )
        for n in range(W_CHUNKS)
    ]

    @pl.when(blk > 0)
    def _():
        pl.semaphore_signal(ready, inc=1, device_id={"blk": blk - 1}, device_id_type=MESH)

    for i in range(FLIGHT):
        @pl.when(i < flight(0))
        def _():
            send(0, i)

    peers(False, entered)

    x_load.start()
    for load in w_loads:
        load.start()

    above = ns + nu - 2 - split - sub

    @pl.when(above > 0)
    def _():
        pl.semaphore_wait(entered, above)

    @pl.when(blk < nb - 1)
    def _():
        pl.semaphore_wait(ready, 1)

    for i in range(FLIGHT):
        @pl.when(i < flight(1))
        def _():
            send(1, i)

    r_load = pltpu.make_async_copy(r_ref, rv, sem_loc.at[1])
    r_load.start()

    def bank_slot(place, e):
        return dnp.at[pl.ds(pl.multiple_of((place * banks + e) * rank, rank), rank)]

    table_loads = [
        pltpu.make_async_copy(src, dst, sem_loc.at[2 + n])
        for n, (src, dst) in enumerate(
            ((ent_any, ent_ref), (rank_any, rank_ref), (ten_any, ten_ref))
        )
    ]
    bank_loads = [
        pltpu.make_async_copy(dn_ref.at[e], bank_slot(blk % group, e), sem_bank.at[e])
        for e in range(banks)
    ]

    @pl.when(in_middle)
    def _():
        for load in bank_loads:
            load.start()

    for load in table_loads:
        load.start()

    def up_slot(bank):
        return upp.at[pl.ds(pl.multiple_of(bank * rank, rank), rank)]

    up_loads = [
        pltpu.make_async_copy(up_ref.at[e], up_slot(split * up_banks + e), sem_up.at[e])
        for e in range(up_banks)
    ]
    for load in up_loads:
        load.start()

    def u_copy(k, e, owner):
        return pltpu.make_async_remote_copy(
            src_ref=up_ref.at[e],
            dst_ref=up_slot(owner * up_banks + e),
            send_sem=usend.at[k - 1, e],
            recv_sem=urecv.at[k - 1, e],
            device_id={"split": lax.rem(split + k, ns)},
            device_id_type=MESH,
        )

    for k in range(1, ns):
        for e in range(up_banks):
            u_copy(k, e, split).start()

    half_lanes = pl.ds(pl.multiple_of(sub * half, half), half)

    def bank_half(place, e, core):
        return dnp.at[
            pl.ds(pl.multiple_of((place * banks + e) * rank, rank), rank),
            pl.ds(pl.multiple_of(core * half, half), half),
        ]

    def b_copy(e, place):
        return pltpu.make_async_remote_copy(
            src_ref=dn_ref.at[e, :, half_lanes],
            dst_ref=bank_half(place, e, sub),
            send_sem=bsend.at[e],
            recv_sem=brecv.at[place, e],
            device_id={"blk": middle},
            device_id_type=MESH,
        )

    def bc_copy(e, place, k, core):
        return pltpu.make_async_remote_copy(
            src_ref=bank_half(place, e, core),
            dst_ref=bank_half(place, e, core),
            send_sem=bcsend.at[k - 1, place, e],
            recv_sem=bcrecv.at[k - 1, place, e],
            device_id={"sub": lax.rem(sub + k, nu)},
            device_id_type=MESH,
        )

    def p_copy(b, src):
        owner = b // per
        return pltpu.make_async_remote_copy(
            src_ref=xs.at[b],
            dst_ref=xr.at[src, b - owner * per],
            send_sem=psend.at[b],
            recv_sem=precv.at[src, b - owner * per],
            device_id={"split": owner},
            device_id_type=MESH,
        )

    def l_copy(b, src):
        owner = b // per
        return pltpu.make_async_remote_copy(
            src_ref=ls.at[b],
            dst_ref=lr.at[src, b - owner * per],
            send_sem=lsend.at[b],
            recv_sem=lrecv.at[src, b - owner * per],
            device_id={"split": owner},
            device_id_type=MESH,
        )

    def g_copy(k, h):
        return pltpu.make_async_remote_copy(
            src_ref=lowx.at[h, sub],
            dst_ref=lowx.at[h, sub],
            send_sem=gsend.at[k - 1],
            recv_sem=grecv.at[h],
            device_id={"blk": lax.rem(blk + k, nb)},
            device_id_type=MESH,
        )

    def f_copy(k, h, core):
        return pltpu.make_async_remote_copy(
            src_ref=lowx.at[h, core],
            dst_ref=lowx.at[h, core],
            send_sem=fsend.at[k - 1, h],
            recv_sem=frecv.at[k - 1, h],
            device_id={"sub": lax.rem(sub + k, nu)},
            device_id_type=MESH,
        )

    def columns(tens):
        n = tens.shape[1]
        return jnp.transpose(jnp.broadcast_to(tens.astype(F32), (8, n)))[:, :1]

    def make_tables():
        for load in table_loads:
            load.wait()
        lanes = lax.broadcasted_iota(jnp.int32, (1, 2 * wide), 1)
        tcol = columns(ten_ref[:, pl.ds(pl.multiple_of(split * own, own), own)])
        table = jnp.zeros((own, 2 * wide), F32)
        for t in range(tenants):
            first = jnp.full((1, 2 * wide), ent_ref[t], jnp.int32) * rank
            line = jnp.where((lanes >= first) & (lanes < first + rank), 1.0, 0.0)
            table = jnp.where(tcol == t, line, table)
        hot[...] = table.astype(hot.dtype)

        @pl.when(in_middle)
        def _():
            lane = lax.broadcasted_iota(jnp.int32, (1, wide), 1)
            tcol = columns(ten_ref[...])
            table = jnp.zeros((total, wide), F32)
            for t in range(tenants):
                live = jnp.full((1, wide), rank_ref[t], jnp.int32)
                slot = jnp.full((1, wide), ent_ref[t], jnp.int32)
                line = jnp.zeros((1, wide), F32)
                for e in range(group * banks):
                    keep = (
                        (lane >= e * rank) & (lane < e * rank + jnp.minimum(live, rank))
                        & (slot == upper * group * banks + e)
                    )
                    line = jnp.where(keep, rank / live.astype(F32), line)
                table = jnp.where(tcol == t, line, table)
            mtab[...] = table

    def finish(b):
        @pl.when(b // per != split)
        def _():
            xs[b] = acc[b].astype(xs.dtype)
            p_copy(b, split).start()

    def own_rows(n):
        if n == 0:
            x_load.wait()
        for m in range(W_CHUNKS):
            if min(m, 2) == n:
                w_loads[m].wait()
        here = slice(n * wrows, (n + 1) * wrows)
        part = jnp.dot(xown[:, here], wv[here, :], preferred_element_type=F32)
        if n == 0:
            acc[blk] = part
        else:
            acc[blk] += part
        if n == W_CHUNKS - 1:
            finish(blk)

    def own_pieces():
        for c in range(nu):
            for q in range(pieces):
                xall[blk, c, q] = xown[:, c * half + q * fc:c * half + (q + 1) * fc]

    def gather(side, i):
        @pl.when((i >= 0) & (i < arrivals(side)))
        def _():
            for k in range(1, nu):
                c_copy(side, i, k, lax.rem(sub - k + nu, nu)).wait_recv()
                c_copy(side, i, k, sub).wait_send()

    def compute(side, i):
        @pl.when((i >= 0) & (i < arrivals(side)))
        def _():
            b, q = order(side, blk, i)
            part = jnp.zeros((rows, cols), F32)
            for c in range(nu):
                at = pl.ds(pl.multiple_of(c * half + q * fc, fc), fc)
                part = part + jnp.dot(xall[b, c, q], wv[at, :], preferred_element_type=F32)

            @pl.when(q == 0)
            def _():
                acc[b] = part

            @pl.when(q != 0)
            def _():
                acc[b] += part

            @pl.when(q == pieces - 1)
            def _():
                finish(b)

    def each_far_bank(body):
        for p in range(group):
            @pl.when(p != blk % group)
            def _():
                for e in range(banks):
                    body(e, p)

    def banks_in():
        for load in bank_loads:
            load.wait()

        def body(e, p):
            b_copy(e, p).wait_recv()
            for k in range(1, nu):
                bc_copy(e, p, k, sub).start()

        each_far_bank(body)

    def banks_shared():
        def body(e, p):
            for k in range(1, nu):
                bc_copy(e, p, k, lax.rem(sub - k + nu, nu)).wait_recv()
                bc_copy(e, p, k, sub).wait_send()

        each_far_bank(body)

    def low_work(blocks):
        part_rows = pl.ds(pl.multiple_of(sub * share, share), share)
        low = jnp.zeros((len(blocks) * share, wide), F32)
        for c in range(nu):
            for q in range(pieces):
                x = jnp.concatenate([xall[b, c, q, part_rows, :] for b in blocks], axis=0)
                d = dnp[:, c * half + q * fc:c * half + (q + 1) * fc]
                low = low + lax.dot_general(
                    x, d, (((1,), (1,)), ((), ())), preferred_element_type=F32
                )
        for m, b in enumerate(blocks):
            mine = low[m * share:(m + 1) * share]

            @pl.when(b // per == split)
            def _():
                lacc[b - split * per] = mine

            @pl.when(b // per != split)
            def _():
                ls[b] = mine
                l_copy(b, split).start()

    def low_early():
        some = 3 if (nb - 1) % 3 == 0 else 1

        @pl.loop(0, (nb - 1) // some)
        def _(n):
            low_work([n * some + m + upper for m in range(some)])

    def low_spread():
        kept = []
        for o in range(per):
            b = split * per + o
            low = lacc[o]
            for k in range(1, ns):
                src = lax.rem(split + k, ns)
                l_copy(b, src).wait_recv()
                low = low + lr[src, o]
            low = low * mtab[pl.ds(pl.multiple_of(b * rows + sub * share, share), share), :]
            kept.append(
                sum(low[:, e * rank:(e + 1) * rank] for e in range(1, wide // rank))
                + low[:, :rank]
            )
        lowx[upper, sub] = jnp.concatenate(kept, axis=1).astype(lowx.dtype)
        for k in range(1, nb):
            g_copy(k, upper).start()

    def low_share():
        for h in range(2):
            @pl.when(jnp.logical_not(in_middle & (upper == h)))
            def _():
                g_copy(1, h).wait_recv()
            for k in range(1, nu):
                f_copy(k, h, sub).start()

    low_tick = group * pieces + 1
    away = jnp.where(upper == 0, middle - blk, blk - middle)
    bank_tick = jnp.maximum(pieces - FLIGHT, (away - 1) * pieces + 1)

    def arrive(side, i):
        @pl.when((i >= 0) & (i < arrivals(side)))
        def _():
            z_copy(side, i, blk).wait_recv()
            for k in range(1, nu):
                c_copy(side, i, k, sub).start()

    @pl.loop(0, ticks)
    def _(t):
        @pl.when((t == low_tick + 1) & in_middle)
        def _():
            low_spread()

        for side in range(2):
            arrive(side, t - 1)

            @pl.when(t + flight(side) < sends(side))
            def _():
                z_copy(side, t, target(side)).wait_send()
                send(side, t + flight(side))

        @pl.when((t == bank_tick) & jnp.logical_not(in_middle))
        def _():
            for e in range(banks):
                b_copy(e, blk % group).start()

        for n in range(W_CHUNKS):
            @pl.when(t == n)
            def _():
                own_rows(n)

        @pl.when(t == W_CHUNKS)
        def _():
            make_tables()

        @pl.when((t == W_CHUNKS + 1) & in_middle)
        def _():
            own_pieces()

        @pl.when((t == low_tick - 4) & in_middle)
        def _():
            banks_in()

        @pl.when((t == low_tick - 3) & in_middle)
        def _():
            banks_shared()

        @pl.when(t == ticks - 1)
        def _():
            low_share()

        for side in range(2):
            gather(side, t - 2)

        @pl.when((t == low_tick) & in_middle)
        def _():
            low_work([jnp.where(upper == 0, nb - 1, 0)])

        for side in range(2):
            compute(side, t - 2)

        @pl.when((t == low_tick - EARLY) & in_middle)
        def _():
            low_early()

    r_load.wait()
    for load in up_loads:
        load.wait()
    for k in range(1, ns):
        for e in range(up_banks):
            u_copy(k, e, lax.rem(split - k + ns, ns)).wait_recv()
    for h in range(2):
        for k in range(1, nu):
            f_copy(k, h, lax.rem(sub - k + nu, nu)).wait_recv()
    low = jnp.concatenate([lowx[0, c] + lowx[1, c] for c in range(nu)], axis=0)
    for o in range(per):
        here = slice(o * rows, (o + 1) * rows)
        low_o = low[:, o * rank:(o + 1) * rank]
        low_o = jnp.concatenate([low_o] * (2 * wide // rank), axis=1) * hot[here, :]
        acc[split * per + o] += rv[here, :].astype(F32) + jnp.dot(
            low_o, upp[...], preferred_element_type=F32
        )

    for side in range(2):
        arrive(side, ticks - 1)
    for i in (ticks - 2, ticks - 1):
        for side in range(2):
            gather(side, i)
            compute(side, i)

    for o in range(per):
        b = split * per + o
        value = acc[b]
        for k in range(1, ns):
            src = lax.rem(split + k, ns)
            p_copy(b, src).wait_recv()
            value = value + xr[src, o].astype(F32)
        o_ref[o * rows:(o + 1) * rows, :] = value.astype(o_ref.dtype)

    for side in range(2):
        for n in range(FLIGHT):
            @pl.when((sends(side) > 0) & (n < flight(side)))
            def _():
                z_copy(side, sends(side) - 1 - n, target(side)).wait_send()
    for k in range(1, ns):
        for e in range(up_banks):
            u_copy(k, e, split).wait_send()

    @pl.when(jnp.logical_not(in_middle))
    def _():
        for e in range(banks):
            b_copy(e, blk % group).wait_send()

    for b in range(nb):
        @pl.when(b // per != split)
        def _():
            p_copy(b, split).wait_send()

            @pl.when(in_middle)
            def _():
                l_copy(b, split).wait_send()

    @pl.when(in_middle)
    def _():
        for k in range(1, nb):
            g_copy(k, upper).wait_send()

    for h in range(2):
        for k in range(1, nu):
            f_copy(k, h, sub).wait_send()


def shards(
    nb, ns, nu,
    attention_output_rows,
    residual,
    output_projection_weight,
    down_adapter_bank,
    up_adapter_bank,
    rollout_row_tenant,
    tenant_bank_entry,
    tenant_live_rank,
):
    rows, feats = attention_output_rows.shape
    own, cols = residual.shape
    banks, rank, _ = down_adapter_bank.shape
    up_banks = up_adapter_bank.shape[0]
    total = rollout_row_tenant.shape[0]
    wide = nb // 2 * banks * rank
    fc = PIECE
    per = own // rows
    pieces = feats // nu // fc
    items = (nb - 1) * pieces
    share = rows // nu
    dma = pltpu.SemaphoreType.DMA
    bf16 = jnp.bfloat16
    any_spec = pl.BlockSpec(memory_space=pltpu.HBM)
    vmem = pl.BlockSpec(memory_space=pltpu.VMEM)
    return pl.pallas_call(
        functools.partial(kernel, nb, ns, nu, fc),
        out_shape=pltpu.VMEM((own, cols), bf16),
        in_specs=[any_spec] * 8,
        out_specs=vmem,
        scratch_shapes=[
            pltpu.SMEM(tenant_bank_entry.shape, jnp.int32),
            pltpu.SMEM(tenant_live_rank.shape, jnp.int32),
            pltpu.VMEM((1, total), jnp.int32),
            pltpu.VMEM((rows, feats), bf16),
            pltpu.VMEM((nb, nu, pieces, rows, fc), bf16),
            pltpu.VMEM((feats, cols), bf16),
            pltpu.VMEM((own, cols), bf16),
            pltpu.VMEM((wide, feats), bf16),
            pltpu.VMEM((2 * wide, cols), bf16),
            pltpu.VMEM((total, wide), F32),
            pltpu.VMEM((nb, rows, cols), F32),
            pltpu.VMEM((nb, rows, cols), bf16),
            pltpu.VMEM((ns, per, rows, cols), bf16),
            pltpu.VMEM((per, share, wide), F32),
            pltpu.VMEM((nb, share, wide), F32),
            pltpu.VMEM((ns, per, share, wide), F32),
            pltpu.VMEM((2, nu, share, per * rank), bf16),
            pltpu.VMEM((own, 2 * wide), bf16),
            dma((5,)),
            dma((W_CHUNKS,)),
            dma((banks,)),
            dma((up_banks,)),
            pltpu.SemaphoreType.REGULAR,
            pltpu.SemaphoreType.REGULAR,
            dma((2, FLIGHT)),
            dma((items,)),
            dma((nu - 1, 2, 2)),
            dma((nu - 1, items)),
            dma((ns - 1, up_banks)),
            dma((ns - 1, up_banks)),
            dma((banks,)),
            dma((nb // 2, banks)),
            dma((nu - 1, nb // 2, banks)),
            dma((nu - 1, nb // 2, banks)),
            dma((nb,)),
            dma((ns, per)),
            dma((nb,)),
            dma((ns, per)),
            dma((nb - 1,)),
            dma((2,)),
            dma((nu - 1, 2)),
            dma((nu - 1, 2)),
        ],
        compiler_params=pltpu.CompilerParams(
            collective_id=0, has_side_effects=True, vmem_limit_bytes=60 * 2**20
        ),
    )(
        tenant_bank_entry,
        tenant_live_rank,
        attention_output_rows,
        residual,
        output_projection_weight,
        down_adapter_bank,
        up_adapter_bank,
        rollout_row_tenant.reshape(1, total),
    )


def solution(mesh):
    in_specs = (
        P(("groups", "blk"), "split"),
        P(("groups", "split"), ("blk", "sub")),
        P("split", ("blk", "sub")),
        P("blk", None, "split"),
        P("split", None, ("blk", "sub")),
        P("groups"),
        P(),
        P(),
    )
    out_specs = P(("groups", "split"), ("blk", "sub"))
    body = functools.partial(
        shards, mesh.shape["blk"], mesh.shape["split"], mesh.shape["sub"]
    )
    return jax.shard_map(body, mesh=mesh, in_specs=in_specs, out_specs=out_specs, check_vma=False)
```

```python
import functools

import jax
import jax.numpy as jnp
from jax import lax
from jax.experimental import pallas as pl
from jax.experimental.pallas import tpu as pltpu
from jax.sharding import PartitionSpec as P

PIECE = 256
FLIGHT = 4
LEAD = (4, 3)
RING = max(FLIGHT, *LEAD)
W_CHUNKS = 4
EARLY = 2
MESH = pl.DeviceIdType.MESH
F32 = jnp.float32


def kernel(
    nb, ns, nu, fc,
    ent_any, rank_any, x_ref, r_ref, w_ref, dn_ref, up_ref, ten_any, o_ref,
    ent_ref, rank_ref, ten_ref, xown, xall, wv, rv, dnp, upp, mtab, acc, xs, xr, lacc, ls, lr, lowx, hot,
    sem_loc, sem_w, sem_bank, sem_up, ready, entered, zsend, zrecv, csend, crecv,
    usend, urecv, bsend, brecv, bcsend, bcrecv, psend, precv, lsend, lrecv, gsend, grecv, fsend, frecv,
):
    blk, split, sub = lax.axis_index("blk"), lax.axis_index("split"), lax.axis_index("sub")
    rows, feats = x_ref.shape
    cols = w_ref.shape[1]
    own = r_ref.shape[0]
    banks, rank = dn_ref.shape[0], dn_ref.shape[1]
    up_banks = up_ref.shape[0]
    wide = dnp.shape[0]
    total = ten_ref.shape[1]
    tenants = ent_ref.shape[0]
    per = own // rows
    half = feats // nu
    pieces = half // fc
    share = rows // nu
    group = nb // 2
    upper = blk // group
    middle = group - 1 + upper
    in_middle = blk == middle
    ticks = (nb - 1) * pieces

    barrier = pltpu.get_barrier_semaphore()

    @pl.when(blk < nb - 1)
    def _():
        pl.semaphore_signal(barrier, inc=1, device_id={"blk": blk + 1}, device_id_type=MESH)

    def peers(upper_ones, sem):
        for axis, n, me in (("split", ns, split), ("sub", nu, sub)):
            for k in range(1, n):
                to = me + k if upper_ones else me - k

                @pl.when(to < n if upper_ones else to >= 0)
                def _():
                    pl.semaphore_signal(
                        sem, inc=1, device_id={axis: jnp.clip(to, 0, n - 1)},
                        device_id_type=MESH,
                    )

    peers(True, barrier)
    below = jnp.where(blk > 0, 1, 0) + split + sub

    @pl.when(below > 0)
    def _():
        pl.semaphore_wait(barrier, below)


    def arrivals(side):
        return (nb - 1 - blk if side == 0 else blk) * pieces

    def sends(side):
        if side == 0:
            return jnp.where(blk > 0, nb - blk, 0) * pieces
        return jnp.where(blk < nb - 1, blk + 1, 0) * pieces

    def is_late(side, to):
        near = jnp.clip(to + 1 - 2 * side, 0, nb - 1)
        return (to == (0 if side == 0 else nb - 1)) & (near // per == split)

    def order(side, to, i):
        sign = 1 - 2 * side
        near = to + sign
        late = is_late(side, to)
        body = (nb - 2) * pieces
        lead = LEAD[side]
        first = i < lead
        last = i >= lead + body
        j = i - lead
        b_late = jnp.where(first | last, near, near + sign * (1 + j // pieces))
        q_late = jnp.where(first, i, jnp.where(last, i - body, lax.rem(j + pieces, pieces)))
        b = jnp.where(late, b_late, near + sign * (i // pieces))
        q = jnp.where(late, q_late, lax.rem(i, pieces))
        return jnp.clip(b, 0, nb - 1), jnp.clip(q, 0, pieces - 1)

    def z_copy(side, i, to, mine=False):
        b, q = order(side, to, i)
        dst = xall.at[b, sub, q]
        src = dst
        if mine:
            src = x_ref.at[:, pl.ds(pl.multiple_of(sub * half + q * fc, fc), fc)]
        return pltpu.make_async_remote_copy(
            src_ref=src,
            dst_ref=dst,
            send_sem=zsend.at[side, lax.rem(i, RING)],
            recv_sem=zrecv.at[i if side == 0 else ticks - 1 - i],
            device_id={"blk": jnp.where(to == blk, lax.rem(blk + 1, nb), jnp.clip(to, 0, nb - 1))},
            device_id_type=MESH,
        )

    def target(side):
        return blk - 1 if side == 0 else blk + 1

    def flight(side):
        return jnp.where(is_late(side, target(side)), LEAD[side], FLIGHT)

    def send(side, i):
        to = target(side)
        b, _ = order(side, to, i)

        @pl.when((i < sends(side)) & (b == blk))
        def _():
            z_copy(side, i, to, True).start()

        @pl.when((i < sends(side)) & (b != blk))
        def _():
            z_copy(side, i, to).start()

    def c_copy(side, i, k, core):
        b, q = order(side, blk, i)
        piece = xall.at[b, core, q]
        return pltpu.make_async_remote_copy(
            src_ref=piece,
            dst_ref=piece,
            send_sem=csend.at[k - 1, side, lax.rem(i, 2)],
            recv_sem=crecv.at[k - 1, side, lax.rem(i, 4)],
            device_id={"sub": lax.rem(sub + k, nu)},
            device_id_type=MESH,
        )

    x_load = pltpu.make_async_copy(x_ref, xown, sem_loc.at[0])
    wrows = feats // W_CHUNKS
    w_loads = [
        pltpu.make_async_copy(
            w_ref.at[pl.ds(n * wrows, wrows)], wv.at[pl.ds(n * wrows, wrows)], sem_w.at[n]
        )
        for n in range(W_CHUNKS)
    ]

    @pl.when(blk > 0)
    def _():
        pl.semaphore_signal(ready, inc=1, device_id={"blk": blk - 1}, device_id_type=MESH)

    for i in range(RING):
        @pl.when(i < flight(0))
        def _():
            send(0, i)

    peers(False, entered)

    x_load.start()
    for load in w_loads:
        load.start()

    above = ns + nu - 2 - split - sub

    @pl.when(above > 0)
    def _():
        pl.semaphore_wait(entered, above)

    @pl.when(blk < nb - 1)
    def _():
        pl.semaphore_wait(ready, 1)

    for i in range(RING):
        @pl.when(i < flight(1))
        def _():
            send(1, i)

    r_load = pltpu.make_async_copy(r_ref, rv, sem_loc.at[1])
    r_load.start()

    def bank_slot(place, e):
        return dnp.at[pl.ds(pl.multiple_of((place * banks + e) * rank, rank), rank)]

    table_loads = [
        pltpu.make_async_copy(src, dst, sem_loc.at[2 + n])
        for n, (src, dst) in enumerate(
            ((ent_any, ent_ref), (rank_any, rank_ref), (ten_any, ten_ref))
        )
    ]
    bank_loads = [
        pltpu.make_async_copy(dn_ref.at[e], bank_slot(blk % group, e), sem_bank.at[e])
        for e in range(banks)
    ]

    @pl.when(in_middle)
    def _():
        for load in bank_loads:
            load.start()

    for load in table_loads:
        load.start()

    def up_slot(bank):
        return upp.at[pl.ds(pl.multiple_of(bank * rank, rank), rank)]

    up_loads = [
        pltpu.make_async_copy(up_ref.at[e], up_slot(split * up_banks + e), sem_up.at[e])
        for e in range(up_banks)
    ]
    for load in up_loads:
        load.start()

    def u_copy(k, e, owner):
        return pltpu.make_async_remote_copy(
            src_ref=up_ref.at[e],
            dst_ref=up_slot(owner * up_banks + e),
            send_sem=usend.at[k - 1, e],
            recv_sem=urecv.at[k - 1, e],
            device_id={"split": lax.rem(split + k, ns)},
            device_id_type=MESH,
        )

    for k in range(1, ns):
        for e in range(up_banks):
            u_copy(k, e, split).start()

    half_lanes = pl.ds(pl.multiple_of(sub * half, half), half)

    def bank_half(place, e, core):
        return dnp.at[
            pl.ds(pl.multiple_of((place * banks + e) * rank, rank), rank),
            pl.ds(pl.multiple_of(core * half, half), half),
        ]

    def b_copy(e, place):
        return pltpu.make_async_remote_copy(
            src_ref=dn_ref.at[e, :, half_lanes],
            dst_ref=bank_half(place, e, sub),
            send_sem=bsend.at[e],
            recv_sem=brecv.at[place, e],
            device_id={"blk": middle},
            device_id_type=MESH,
        )

    def bc_copy(e, place, k, core):
        return pltpu.make_async_remote_copy(
            src_ref=bank_half(place, e, core),
            dst_ref=bank_half(place, e, core),
            send_sem=bcsend.at[k - 1, place, e],
            recv_sem=bcrecv.at[k - 1, place, e],
            device_id={"sub": lax.rem(sub + k, nu)},
            device_id_type=MESH,
        )

    def p_copy(b, src):
        owner = b // per
        return pltpu.make_async_remote_copy(
            src_ref=xs.at[b],
            dst_ref=xr.at[src, b - owner * per],
            send_sem=psend.at[b],
            recv_sem=precv.at[src, b - owner * per],
            device_id={"split": owner},
            device_id_type=MESH,
        )

    def l_copy(b, src):
        owner = b // per
        return pltpu.make_async_remote_copy(
            src_ref=ls.at[b],
            dst_ref=lr.at[src, b - owner * per],
            send_sem=lsend.at[b],
            recv_sem=lrecv.at[src, b - owner * per],
            device_id={"split": owner},
            device_id_type=MESH,
        )

    def g_copy(k, h):
        return pltpu.make_async_remote_copy(
            src_ref=lowx.at[h, sub],
            dst_ref=lowx.at[h, sub],
            send_sem=gsend.at[k - 1],
            recv_sem=grecv.at[h],
            device_id={"blk": lax.rem(blk + k, nb)},
            device_id_type=MESH,
        )

    def f_copy(k, h, core):
        return pltpu.make_async_remote_copy(
            src_ref=lowx.at[h, core],
            dst_ref=lowx.at[h, core],
            send_sem=fsend.at[k - 1, h],
            recv_sem=frecv.at[k - 1, h],
            device_id={"sub": lax.rem(sub + k, nu)},
            device_id_type=MESH,
        )

    def columns(tens):
        n = tens.shape[1]
        return jnp.transpose(jnp.broadcast_to(tens.astype(F32), (8, n)))[:, :1]

    def make_tables():
        for load in table_loads:
            load.wait()
        lanes = lax.broadcasted_iota(jnp.int32, (1, 2 * wide), 1)
        tcol = columns(ten_ref[:, pl.ds(pl.multiple_of(split * own, own), own)])
        table = jnp.zeros((own, 2 * wide), F32)
        for t in range(tenants):
            first = jnp.full((1, 2 * wide), ent_ref[t], jnp.int32) * rank
            line = jnp.where((lanes >= first) & (lanes < first + rank), 1.0, 0.0)
            table = jnp.where(tcol == t, line, table)
        hot[...] = table.astype(hot.dtype)

        @pl.when(in_middle)
        def _():
            lane = lax.broadcasted_iota(jnp.int32, (1, wide), 1)
            tcol = columns(ten_ref[...])
            table = jnp.zeros((total, wide), F32)
            for t in range(tenants):
                live = jnp.full((1, wide), rank_ref[t], jnp.int32)
                slot = jnp.full((1, wide), ent_ref[t], jnp.int32)
                line = jnp.zeros((1, wide), F32)
                for e in range(group * banks):
                    keep = (
                        (lane >= e * rank) & (lane < e * rank + jnp.minimum(live, rank))
                        & (slot == upper * group * banks + e)
                    )
                    line = jnp.where(keep, rank / live.astype(F32), line)
                table = jnp.where(tcol == t, line, table)
            mtab[...] = table

    def finish(b):
        @pl.when(b // per != split)
        def _():
            xs[b] = acc[b].astype(xs.dtype)
            p_copy(b, split).start()

    def own_rows(n):
        if n == 0:
            x_load.wait()
        for m in range(W_CHUNKS):
            if min(m, 2) == n:
                w_loads[m].wait()
        here = slice(n * wrows, (n + 1) * wrows)
        part = jnp.dot(xown[:, here], wv[here, :], preferred_element_type=F32)
        if n == 0:
            acc[blk] = part
        else:
            acc[blk] += part
        if n == W_CHUNKS - 1:
            finish(blk)

    def own_pieces():
        for c in range(nu):
            for q in range(pieces):
                xall[blk, c, q] = xown[:, c * half + q * fc:c * half + (q + 1) * fc]

    def gather(side, i):
        @pl.when((i >= 0) & (i < arrivals(side)))
        def _():
            for k in range(1, nu):
                c_copy(side, i, k, lax.rem(sub - k + nu, nu)).wait_recv()
                c_copy(side, i, k, sub).wait_send()

    def compute(side, i, whole=True):
        @pl.when((i >= 0) & (i < arrivals(side)))
        def _():
            b, q = order(side, blk, i)
            part = jnp.zeros((rows, cols), F32)
            for n in range(nu):
                c = n if whole else lax.rem(sub + n, nu)
                if not whole and n == 1:
                    gather(side, i)
                at = pl.ds(pl.multiple_of(c * half + q * fc, fc), fc)
                part = part + jnp.dot(xall[b, c, q], wv[at, :], preferred_element_type=F32)

            @pl.when(q == 0)
            def _():
                acc[b] = part

            @pl.when(q != 0)
            def _():
                acc[b] += part

            @pl.when(q == pieces - 1)
            def _():
                finish(b)

    def each_far_bank(body):
        for p in range(group):
            @pl.when(p != blk % group)
            def _():
                for e in range(banks):
                    body(e, p)

    def banks_in():
        for load in bank_loads:
            load.wait()

        def body(e, p):
            b_copy(e, p).wait_recv()
            for k in range(1, nu):
                bc_copy(e, p, k, sub).start()

        each_far_bank(body)

    def banks_shared():
        def body(e, p):
            for k in range(1, nu):
                bc_copy(e, p, k, lax.rem(sub - k + nu, nu)).wait_recv()
                bc_copy(e, p, k, sub).wait_send()

        each_far_bank(body)

    def low_work(blocks):
        part_rows = pl.ds(pl.multiple_of(sub * share, share), share)
        low = jnp.zeros((len(blocks) * share, wide), F32)
        for c in range(nu):
            for q in range(pieces):
                x = jnp.concatenate([xall[b, c, q, part_rows, :] for b in blocks], axis=0)
                d = dnp[:, c * half + q * fc:c * half + (q + 1) * fc]
                low = low + lax.dot_general(
                    x, d, (((1,), (1,)), ((), ())), preferred_element_type=F32
                )
        for m, b in enumerate(blocks):
            mine = low[m * share:(m + 1) * share]

            @pl.when(b // per == split)
            def _():
                lacc[b - split * per] = mine

            @pl.when(b // per != split)
            def _():
                ls[b] = mine
                l_copy(b, split).start()

    def low_early():
        some = 3 if (nb - 1) % 3 == 0 else 1

        @pl.loop(0, (nb - 1) // some)
        def _(n):
            low_work([n * some + m + upper for m in range(some)])

    def low_spread():
        kept = []
        for o in range(per):
            b = split * per + o
            low = lacc[o]
            for k in range(1, ns):
                src = lax.rem(split + k, ns)
                l_copy(b, src).wait_recv()
                low = low + lr[src, o]
            low = low * mtab[pl.ds(pl.multiple_of(b * rows + sub * share, share), share), :]
            kept.append(
                sum(low[:, e * rank:(e + 1) * rank] for e in range(1, wide // rank))
                + low[:, :rank]
            )
        lowx[upper, sub] = jnp.concatenate(kept, axis=1).astype(lowx.dtype)
        for k in range(1, nb):
            g_copy(k, upper).start()

    def low_share():
        for h in range(2):
            @pl.when(jnp.logical_not(in_middle & (upper == h)))
            def _():
                g_copy(1, h).wait_recv()
            for k in range(1, nu):
                f_copy(k, h, sub).start()

    low_tick = group * pieces + 1
    away = jnp.where(upper == 0, middle - blk, blk - middle)
    bank_tick = jnp.maximum(pieces - FLIGHT + 1, (away - 1) * pieces + 1)

    def arrive(side, i):
        @pl.when((i >= 0) & (i < arrivals(side)))
        def _():
            z_copy(side, i, blk).wait_recv()
            for k in range(1, nu):
                c_copy(side, i, k, sub).start()

    @pl.loop(0, ticks)
    def _(t):
        @pl.when((t == low_tick + 1) & in_middle)
        def _():
            low_spread()

        for side in range(2):
            arrive(side, t - 1)

            @pl.when((t >= 1) & (t - 1 + flight(side) < sends(side)))
            def _():
                z_copy(side, t - 1, target(side)).wait_send()
                send(side, t - 1 + flight(side))

        @pl.when((t == bank_tick) & jnp.logical_not(in_middle))
        def _():
            for e in range(banks):
                b_copy(e, blk % group).start()

        for n in range(W_CHUNKS):
            @pl.when(t == n)
            def _():
                own_rows(n)

        @pl.when(t == W_CHUNKS)
        def _():
            make_tables()

        @pl.when((t == W_CHUNKS + 1) & in_middle)
        def _():
            own_pieces()

        @pl.when((t == low_tick - 4) & in_middle)
        def _():
            banks_in()

        @pl.when((t == low_tick - 3) & in_middle)
        def _():
            banks_shared()

        @pl.when(t == ticks - 1)
        def _():
            low_share()

        for side in range(2):
            gather(side, t - 2)

        @pl.when((t == low_tick) & in_middle)
        def _():
            low_work([jnp.where(upper == 0, nb - 1, 0)])

        for side in range(2):
            compute(side, t - 2)

        @pl.when((t == low_tick - EARLY) & in_middle)
        def _():
            low_early()

    for side in range(2):
        arrive(side, ticks - 1)

    r_load.wait()
    for load in up_loads:
        load.wait()
    for k in range(1, ns):
        for e in range(up_banks):
            u_copy(k, e, lax.rem(split - k + ns, ns)).wait_recv()
    for h in range(2):
        for k in range(1, nu):
            f_copy(k, h, lax.rem(sub - k + nu, nu)).wait_recv()
    low = jnp.concatenate([lowx[0, c] + lowx[1, c] for c in range(nu)], axis=0)
    for o in range(per):
        here = slice(o * rows, (o + 1) * rows)
        low_o = low[:, o * rank:(o + 1) * rank]
        low_o = jnp.concatenate([low_o] * (2 * wide // rank), axis=1) * hot[here, :]
        acc[split * per + o] += rv[here, :].astype(F32) + jnp.dot(
            low_o, upp[...], preferred_element_type=F32
        )

    for side in range(2):
        gather(side, ticks - 2)
        compute(side, ticks - 2)
    for side in range(2):
        compute(side, ticks - 1, whole=False)

    for o in range(per):
        b = split * per + o
        value = acc[b]
        for k in range(1, ns):
            src = lax.rem(split + k, ns)
            p_copy(b, src).wait_recv()
            value = value + xr[src, o].astype(F32)
        o_ref[o * rows:(o + 1) * rows, :] = value.astype(o_ref.dtype)

    for side in range(2):
        for n in range(RING):
            @pl.when((sends(side) > 0) & (n < flight(side)))
            def _():
                z_copy(side, sends(side) - 1 - n, target(side)).wait_send()
    for k in range(1, ns):
        for e in range(up_banks):
            u_copy(k, e, split).wait_send()

    @pl.when(jnp.logical_not(in_middle))
    def _():
        for e in range(banks):
            b_copy(e, blk % group).wait_send()

    for b in range(nb):
        @pl.when(b // per != split)
        def _():
            p_copy(b, split).wait_send()

            @pl.when(in_middle)
            def _():
                l_copy(b, split).wait_send()

    @pl.when(in_middle)
    def _():
        for k in range(1, nb):
            g_copy(k, upper).wait_send()

    for h in range(2):
        for k in range(1, nu):
            f_copy(k, h, sub).wait_send()


def shards(
    nb, ns, nu,
    attention_output_rows,
    residual,
    output_projection_weight,
    down_adapter_bank,
    up_adapter_bank,
    rollout_row_tenant,
    tenant_bank_entry,
    tenant_live_rank,
):
    rows, feats = attention_output_rows.shape
    own, cols = residual.shape
    banks, rank, _ = down_adapter_bank.shape
    up_banks = up_adapter_bank.shape[0]
    total = rollout_row_tenant.shape[0]
    wide = nb // 2 * banks * rank
    fc = PIECE
    per = own // rows
    pieces = feats // nu // fc
    items = (nb - 1) * pieces
    share = rows // nu
    dma = pltpu.SemaphoreType.DMA
    bf16 = jnp.bfloat16
    any_spec = pl.BlockSpec(memory_space=pltpu.HBM)
    vmem = pl.BlockSpec(memory_space=pltpu.VMEM)
    return pl.pallas_call(
        functools.partial(kernel, nb, ns, nu, fc),
        out_shape=pltpu.VMEM((own, cols), bf16),
        in_specs=[any_spec] * 8,
        out_specs=vmem,
        scratch_shapes=[
            pltpu.SMEM(tenant_bank_entry.shape, jnp.int32),
            pltpu.SMEM(tenant_live_rank.shape, jnp.int32),
            pltpu.VMEM((1, total), jnp.int32),
            pltpu.VMEM((rows, feats), bf16),
            pltpu.VMEM((nb, nu, pieces, rows, fc), bf16),
            pltpu.VMEM((feats, cols), bf16),
            pltpu.VMEM((own, cols), bf16),
            pltpu.VMEM((wide, feats), bf16),
            pltpu.VMEM((2 * wide, cols), bf16),
            pltpu.VMEM((total, wide), F32),
            pltpu.VMEM((nb, rows, cols), F32),
            pltpu.VMEM((nb, rows, cols), bf16),
            pltpu.VMEM((ns, per, rows, cols), bf16),
            pltpu.VMEM((per, share, wide), F32),
            pltpu.VMEM((nb, share, wide), F32),
            pltpu.VMEM((ns, per, share, wide), F32),
            pltpu.VMEM((2, nu, share, per * rank), bf16),
            pltpu.VMEM((own, 2 * wide), bf16),
            dma((5,)),
            dma((W_CHUNKS,)),
            dma((banks,)),
            dma((up_banks,)),
            pltpu.SemaphoreType.REGULAR,
            pltpu.SemaphoreType.REGULAR,
            dma((2, RING)),
            dma((items,)),
            dma((nu - 1, 2, 2)),
            dma((nu - 1, 2, 4)),
            dma((ns - 1, up_banks)),
            dma((ns - 1, up_banks)),
            dma((banks,)),
            dma((nb // 2, banks)),
            dma((nu - 1, nb // 2, banks)),
            dma((nu - 1, nb // 2, banks)),
            dma((nb,)),
            dma((ns, per)),
            dma((nb,)),
            dma((ns, per)),
            dma((nb - 1,)),
            dma((2,)),
            dma((nu - 1, 2)),
            dma((nu - 1, 2)),
        ],
        compiler_params=pltpu.CompilerParams(
            collective_id=0, has_side_effects=True, vmem_limit_bytes=60 * 2**20
        ),
    )(
        tenant_bank_entry,
        tenant_live_rank,
        attention_output_rows,
        residual,
        output_projection_weight,
        down_adapter_bank,
        up_adapter_bank,
        rollout_row_tenant.reshape(1, total),
    )


def solution(mesh):
    in_specs = (
        P(("groups", "blk"), "split"),
        P(("groups", "split"), ("blk", "sub")),
        P("split", ("blk", "sub")),
        P("blk", None, "split"),
        P("split", None, ("blk", "sub")),
        P("groups"),
        P(),
        P(),
    )
    out_specs = P(("groups", "split"), ("blk", "sub"))
    body = functools.partial(
        shards, mesh.shape["blk"], mesh.shape["split"], mesh.shape["sub"]
    )
    return jax.shard_map(body, mesh=mesh, in_specs=in_specs, out_specs=out_specs, check_vma=False)
```

```python
import functools

import jax
import jax.numpy as jnp
from jax import lax
from jax.experimental import pallas as pl
from jax.experimental.pallas import tpu as pltpu
from jax.sharding import PartitionSpec as P

PIECE = 256
FLIGHT = 4
LEAD = (4, 3)
RING = max(FLIGHT, *LEAD)
W_CHUNKS = 4
EARLY = 2
MESH = pl.DeviceIdType.MESH
F32 = jnp.float32


def kernel(
    nb, ns, nu, fc,
    ent_any, rank_any, x_ref, r_ref, w_ref, dn_ref, up_ref, ten_any, o_ref,
    ent_ref, rank_ref, ten_ref, xown, xall, wv, rv, dnp, upp, mtab, acc, xs, xr, lacc, ls, lr, lowx, hot,
    sem_loc, sem_w, sem_bank, ready, entered, zsend, zrecv, csend, crecv,
    usend, urecv, bsend, brecv, bcsend, bcrecv, psend, precv, lsend, lrecv, gsend, grecv, fsend, frecv,
):
    blk, split, sub = lax.axis_index("blk"), lax.axis_index("split"), lax.axis_index("sub")
    rows, feats = x_ref.shape
    cols = w_ref.shape[1]
    own = r_ref.shape[0]
    banks, rank = dn_ref.shape[0], dn_ref.shape[1]
    up_banks = up_ref.shape[0]
    wide = dnp.shape[0]
    total = ten_ref.shape[1]
    tenants = ent_ref.shape[0]
    per = own // rows
    half = feats // nu
    pieces = half // fc
    share = rows // nu
    group = nb // 2
    upper = blk // group
    middle = group - 1 + upper
    in_middle = blk == middle
    ticks = (nb - 1) * pieces

    barrier = pltpu.get_barrier_semaphore()

    @pl.when(blk < nb - 1)
    def _():
        pl.semaphore_signal(barrier, inc=1, device_id={"blk": blk + 1}, device_id_type=MESH)

    def peers(upper_ones, sem):
        for axis, n, me in (("split", ns, split), ("sub", nu, sub)):
            for k in range(1, n):
                to = me + k if upper_ones else me - k

                @pl.when(to < n if upper_ones else to >= 0)
                def _():
                    pl.semaphore_signal(
                        sem, inc=1, device_id={axis: jnp.clip(to, 0, n - 1)},
                        device_id_type=MESH,
                    )

    peers(True, barrier)
    below = jnp.where(blk > 0, 1, 0) + split + sub

    @pl.when(below > 0)
    def _():
        pl.semaphore_wait(barrier, below)


    def arrivals(side):
        return (nb - 1 - blk if side == 0 else blk) * pieces

    def sends(side):
        if side == 0:
            return jnp.where(blk > 0, nb - blk, 0) * pieces
        return jnp.where(blk < nb - 1, blk + 1, 0) * pieces

    def is_late(side, to):
        near = jnp.clip(to + 1 - 2 * side, 0, nb - 1)
        return (to == (0 if side == 0 else nb - 1)) & (near // per == split)

    def order(side, to, i):
        sign = 1 - 2 * side
        near = to + sign
        late = is_late(side, to)
        body = (nb - 2) * pieces
        lead = LEAD[side]
        first = i < lead
        last = i >= lead + body
        j = i - lead
        b_late = jnp.where(first | last, near, near + sign * (1 + j // pieces))
        q_late = jnp.where(first, i, jnp.where(last, i - body, lax.rem(j + pieces, pieces)))
        b = jnp.where(late, b_late, near + sign * (i // pieces))
        q = jnp.where(late, q_late, lax.rem(i, pieces))
        return jnp.clip(b, 0, nb - 1), jnp.clip(q, 0, pieces - 1)

    def z_copy(side, i, to, mine=False):
        b, q = order(side, to, i)
        dst = xall.at[b, sub, q]
        src = dst
        if mine:
            src = x_ref.at[:, pl.ds(pl.multiple_of(sub * half + q * fc, fc), fc)]
        return pltpu.make_async_remote_copy(
            src_ref=src,
            dst_ref=dst,
            send_sem=zsend.at[side, lax.rem(i, RING)],
            recv_sem=zrecv.at[i if side == 0 else ticks - 1 - i],
            device_id={"blk": jnp.where(to == blk, lax.rem(blk + 1, nb), jnp.clip(to, 0, nb - 1))},
            device_id_type=MESH,
        )

    def target(side):
        return blk - 1 if side == 0 else blk + 1

    def flight(side):
        return jnp.where(is_late(side, target(side)), LEAD[side], FLIGHT)

    def send(side, i):
        to = target(side)
        b, _ = order(side, to, i)

        @pl.when((i < sends(side)) & (b == blk))
        def _():
            z_copy(side, i, to, True).start()

        @pl.when((i < sends(side)) & (b != blk))
        def _():
            z_copy(side, i, to).start()

    def c_copy(side, i, k, core):
        b, q = order(side, blk, i)
        piece = xall.at[b, core, q]
        return pltpu.make_async_remote_copy(
            src_ref=piece,
            dst_ref=piece,
            send_sem=csend.at[k - 1, side, lax.rem(i, 2)],
            recv_sem=crecv.at[k - 1, side, lax.rem(i, 4)],
            device_id={"sub": lax.rem(sub + k, nu)},
            device_id_type=MESH,
        )

    x_load = pltpu.make_async_copy(x_ref, xown, sem_loc.at[0])
    wrows = feats // W_CHUNKS
    w_loads = [
        pltpu.make_async_copy(
            w_ref.at[pl.ds(n * wrows, wrows)], wv.at[pl.ds(n * wrows, wrows)], sem_w.at[n]
        )
        for n in range(W_CHUNKS)
    ]

    @pl.when(blk > 0)
    def _():
        pl.semaphore_signal(ready, inc=1, device_id={"blk": blk - 1}, device_id_type=MESH)

    for i in range(RING):
        @pl.when(i < flight(0))
        def _():
            send(0, i)

    peers(False, entered)

    x_load.start()
    for load in w_loads:
        load.start()

    above = ns + nu - 2 - split - sub

    @pl.when(above > 0)
    def _():
        pl.semaphore_wait(entered, above)

    @pl.when(blk < nb - 1)
    def _():
        pl.semaphore_wait(ready, 1)

    for i in range(RING):
        @pl.when(i < flight(1))
        def _():
            send(1, i)

    r_load = pltpu.make_async_copy(r_ref, rv, sem_loc.at[1])
    r_load.start()

    def bank_slot(place, e):
        return dnp.at[pl.ds(pl.multiple_of((place * banks + e) * rank, rank), rank)]

    table_loads = [
        pltpu.make_async_copy(src, dst, sem_loc.at[1])
        for src, dst in ((ent_any, ent_ref), (rank_any, rank_ref), (ten_any, ten_ref))
    ]
    bank_loads = [
        pltpu.make_async_copy(dn_ref.at[e], bank_slot(blk % group, e), sem_bank.at[e])
        for e in range(banks)
    ]

    @pl.when(in_middle)
    def _():
        for load in bank_loads:
            load.start()

    for load in table_loads:
        load.start()

    def up_slot(bank):
        return upp.at[pl.ds(pl.multiple_of(bank * rank, rank), rank)]

    up_loads = [
        pltpu.make_async_copy(up_ref.at[e], up_slot(split * up_banks + e), sem_loc.at[1])
        for e in range(up_banks)
    ]
    for load in up_loads:
        load.start()

    def u_copy(k, e, owner):
        return pltpu.make_async_remote_copy(
            src_ref=up_ref.at[e],
            dst_ref=up_slot(owner * up_banks + e),
            send_sem=usend.at[k - 1, e],
            recv_sem=urecv.at[k - 1, e],
            device_id={"split": lax.rem(split + k, ns)},
            device_id_type=MESH,
        )

    for k in range(1, ns):
        for e in range(up_banks):
            u_copy(k, e, split).start()

    half_lanes = pl.ds(pl.multiple_of(sub * half, half), half)

    def bank_half(place, e, core):
        return dnp.at[
            pl.ds(pl.multiple_of((place * banks + e) * rank, rank), rank),
            pl.ds(pl.multiple_of(core * half, half), half),
        ]

    def b_copy(e, place):
        return pltpu.make_async_remote_copy(
            src_ref=dn_ref.at[e, :, half_lanes],
            dst_ref=bank_half(place, e, sub),
            send_sem=bsend.at[e],
            recv_sem=brecv.at[place, e],
            device_id={"blk": middle},
            device_id_type=MESH,
        )

    def bc_copy(e, place, k, core):
        return pltpu.make_async_remote_copy(
            src_ref=bank_half(place, e, core),
            dst_ref=bank_half(place, e, core),
            send_sem=bcsend.at[k - 1, place, e],
            recv_sem=bcrecv.at[k - 1, place, e],
            device_id={"sub": lax.rem(sub + k, nu)},
            device_id_type=MESH,
        )

    def p_copy(b, src):
        owner = b // per
        return pltpu.make_async_remote_copy(
            src_ref=xs.at[b],
            dst_ref=xr.at[src, b - owner * per],
            send_sem=psend.at[b],
            recv_sem=precv.at[lax.rem(src - owner + ns, ns) - 1, b - owner * per],
            device_id={"split": owner},
            device_id_type=MESH,
        )

    def l_copy(b, src):
        owner = b // per
        return pltpu.make_async_remote_copy(
            src_ref=ls.at[b],
            dst_ref=lr.at[src, b - owner * per],
            send_sem=lsend.at[b],
            recv_sem=lrecv.at[lax.rem(src - owner + ns, ns) - 1, b - owner * per],
            device_id={"split": owner},
            device_id_type=MESH,
        )

    def g_copy(k, h):
        return pltpu.make_async_remote_copy(
            src_ref=lowx.at[h, sub],
            dst_ref=lowx.at[h, sub],
            send_sem=gsend.at[k - 1],
            recv_sem=grecv.at[h],
            device_id={"blk": lax.rem(blk + k, nb)},
            device_id_type=MESH,
        )

    def f_copy(k, h, core):
        return pltpu.make_async_remote_copy(
            src_ref=lowx.at[h, core],
            dst_ref=lowx.at[h, core],
            send_sem=fsend.at[k - 1, h],
            recv_sem=frecv.at[k - 1, h],
            device_id={"sub": lax.rem(sub + k, nu)},
            device_id_type=MESH,
        )

    def columns(tens):
        n = tens.shape[1]
        return jnp.transpose(jnp.broadcast_to(tens.astype(F32), (8, n)))[:, :1]

    def make_tables():
        for load in table_loads + up_loads + [r_load]:
            load.wait()
        lanes = lax.broadcasted_iota(jnp.int32, (1, 2 * wide), 1)
        tcol = columns(ten_ref[:, pl.ds(pl.multiple_of(split * own, own), own)])
        table = jnp.zeros((own, 2 * wide), F32)
        for t in range(tenants):
            first = jnp.full((1, 2 * wide), ent_ref[t], jnp.int32) * rank
            line = jnp.where((lanes >= first) & (lanes < first + rank), 1.0, 0.0)
            table = jnp.where(tcol == t, line, table)
        hot[...] = table.astype(hot.dtype)

        @pl.when(in_middle)
        def _():
            lane = lax.broadcasted_iota(jnp.int32, (1, wide), 1)
            tcol = columns(ten_ref[...])
            table = jnp.zeros((total, wide), F32)
            for t in range(tenants):
                live = jnp.full((1, wide), rank_ref[t], jnp.int32)
                slot = jnp.full((1, wide), ent_ref[t], jnp.int32)
                line = jnp.zeros((1, wide), F32)
                for e in range(group * banks):
                    keep = (
                        (lane >= e * rank) & (lane < e * rank + jnp.minimum(live, rank))
                        & (slot == upper * group * banks + e)
                    )
                    line = jnp.where(keep, rank / live.astype(F32), line)
                table = jnp.where(tcol == t, line, table)
            mtab[...] = table

    def finish(b):
        @pl.when(b // per != split)
        def _():
            xs[b] = acc[b].astype(xs.dtype)
            p_copy(b, split).start()

    def own_rows(n):
        if n == 0:
            x_load.wait()
        for m in range(W_CHUNKS):
            if min(m, 2) == n:
                w_loads[m].wait()
        here = slice(n * wrows, (n + 1) * wrows)
        part = jnp.dot(xown[:, here], wv[here, :], preferred_element_type=F32)
        if n == 0:
            acc[blk] = part
        else:
            acc[blk] += part
        if n == W_CHUNKS - 1:
            finish(blk)

    def own_pieces():
        for c in range(nu):
            for q in range(pieces):
                xall[blk, c, q] = xown[:, c * half + q * fc:c * half + (q + 1) * fc]

    def gather(side, i):
        @pl.when((i >= 0) & (i < arrivals(side)))
        def _():
            for k in range(1, nu):
                c_copy(side, i, k, lax.rem(sub - k + nu, nu)).wait_recv()
                c_copy(side, i, k, sub).wait_send()

    def compute(side, i, whole=True):
        @pl.when((i >= 0) & (i < arrivals(side)))
        def _():
            b, q = order(side, blk, i)
            part = jnp.zeros((rows, cols), F32)
            for n in range(nu):
                c = n if whole else lax.rem(sub + n, nu)
                if not whole and n == 1:
                    gather(side, i)
                at = pl.ds(pl.multiple_of(c * half + q * fc, fc), fc)
                part = part + jnp.dot(xall[b, c, q], wv[at, :], preferred_element_type=F32)

            @pl.when(q == 0)
            def _():
                acc[b] = part

            @pl.when(q != 0)
            def _():
                acc[b] += part

            @pl.when(q == pieces - 1)
            def _():
                finish(b)

    def each_far_bank(body):
        for p in range(group):
            @pl.when(p != blk % group)
            def _():
                for e in range(banks):
                    body(e, p)

    def banks_in():
        for load in bank_loads:
            load.wait()

        def body(e, p):
            b_copy(e, p).wait_recv()
            for k in range(1, nu):
                bc_copy(e, p, k, sub).start()

        each_far_bank(body)

    def banks_shared():
        def body(e, p):
            for k in range(1, nu):
                bc_copy(e, p, k, lax.rem(sub - k + nu, nu)).wait_recv()
                bc_copy(e, p, k, sub).wait_send()

        each_far_bank(body)

    def low_work(blocks):
        part_rows = pl.ds(pl.multiple_of(sub * share, share), share)
        low = jnp.zeros((len(blocks) * share, wide), F32)
        for c in range(nu):
            for q in range(pieces):
                x = jnp.concatenate([xall[b, c, q, part_rows, :] for b in blocks], axis=0)
                d = dnp[:, c * half + q * fc:c * half + (q + 1) * fc]
                low = low + lax.dot_general(
                    x, d, (((1,), (1,)), ((), ())), preferred_element_type=F32
                )
        for m, b in enumerate(blocks):
            mine = low[m * share:(m + 1) * share]

            @pl.when(b // per == split)
            def _():
                lacc[b - split * per] = mine

            @pl.when(b // per != split)
            def _():
                ls[b] = mine
                l_copy(b, split).start()

    def low_early():
        some = 3 if (nb - 1) % 3 == 0 else 1

        @pl.loop(0, (nb - 1) // some)
        def _(n):
            low_work([n * some + m + upper for m in range(some)])

    def low_spread():
        kept = []
        for o in range(per):
            b = split * per + o
            low = lacc[o]
            for k in range(1, ns):
                src = lax.rem(split + k, ns)
                l_copy(b, src).wait_recv()
                low = low + lr[src, o]
            low = low * mtab[pl.ds(pl.multiple_of(b * rows + sub * share, share), share), :]
            kept.append(
                sum(low[:, e * rank:(e + 1) * rank] for e in range(1, wide // rank))
                + low[:, :rank]
            )
        lowx[upper, sub] = jnp.concatenate(kept, axis=1).astype(lowx.dtype)
        for k in range(1, nb):
            g_copy(k, upper).start()

    def low_share():
        for h in range(2):
            @pl.when(jnp.logical_not(in_middle & (upper == h)))
            def _():
                g_copy(1, h).wait_recv()
            for k in range(1, nu):
                f_copy(k, h, sub).start()

    low_tick = group * pieces + 1
    away = jnp.where(upper == 0, middle - blk, blk - middle)
    bank_tick = jnp.maximum(pieces - FLIGHT + 1, (away - 1) * pieces + 1)

    def arrive(side, i):
        @pl.when((i >= 0) & (i < arrivals(side)))
        def _():
            z_copy(side, i, blk).wait_recv()
            for k in range(1, nu):
                c_copy(side, i, k, sub).start()

    @pl.loop(0, ticks)
    def _(t):
        @pl.when((t == low_tick + 1) & in_middle)
        def _():
            low_spread()

        for side in range(2):
            arrive(side, t - 1)

            @pl.when((t >= 1) & (t - 1 + flight(side) < sends(side)))
            def _():
                z_copy(side, t - 1, target(side)).wait_send()
                send(side, t - 1 + flight(side))

        @pl.when((t == bank_tick) & jnp.logical_not(in_middle))
        def _():
            for e in range(banks):
                b_copy(e, blk % group).start()

        for n in range(W_CHUNKS):
            @pl.when(t == n)
            def _():
                own_rows(n)

        @pl.when(t == W_CHUNKS)
        def _():
            make_tables()

        @pl.when((t == W_CHUNKS + 1) & in_middle)
        def _():
            own_pieces()

        @pl.when((t == low_tick - 4) & in_middle)
        def _():
            banks_in()

        @pl.when((t == low_tick - 3) & in_middle)
        def _():
            banks_shared()

        @pl.when(t == ticks - 1)
        def _():
            low_share()

        for side in range(2):
            gather(side, t - 2)

        @pl.when((t == low_tick) & in_middle)
        def _():
            low_work([jnp.where(upper == 0, nb - 1, 0)])

        for side in range(2):
            compute(side, t - 2)

        @pl.when((t == low_tick - EARLY) & in_middle)
        def _():
            low_early()

    for side in range(2):
        arrive(side, ticks - 1)

    for k in range(1, ns):
        for e in range(up_banks):
            u_copy(k, e, lax.rem(split - k + ns, ns)).wait_recv()
    for h in range(2):
        for k in range(1, nu):
            f_copy(k, h, lax.rem(sub - k + nu, nu)).wait_recv()
    low = jnp.concatenate([lowx[0, c] + lowx[1, c] for c in range(nu)], axis=0)
    for o in range(per):
        here = slice(o * rows, (o + 1) * rows)
        low_o = low[:, o * rank:(o + 1) * rank]
        low_o = jnp.concatenate([low_o] * (2 * wide // rank), axis=1) * hot[here, :]
        acc[split * per + o] += rv[here, :].astype(F32) + jnp.dot(
            low_o, upp[...], preferred_element_type=F32
        )

    for side in range(2):
        gather(side, ticks - 2)
        compute(side, ticks - 2)
    for side in range(2):
        compute(side, ticks - 1, whole=False)

    for o in range(per):
        b = split * per + o
        value = acc[b]
        for k in range(1, ns):
            src = lax.rem(split + k, ns)
            p_copy(b, src).wait_recv()
            value = value + xr[src, o].astype(F32)
        o_ref[o * rows:(o + 1) * rows, :] = value.astype(o_ref.dtype)

    for side in range(2):
        for n in range(RING):
            @pl.when((sends(side) > 0) & (n < flight(side)))
            def _():
                z_copy(side, sends(side) - 1 - n, target(side)).wait_send()
    for k in range(1, ns):
        for e in range(up_banks):
            u_copy(k, e, split).wait_send()

    @pl.when(jnp.logical_not(in_middle))
    def _():
        for e in range(banks):
            b_copy(e, blk % group).wait_send()

    for b in range(nb):
        @pl.when(b // per != split)
        def _():
            p_copy(b, split).wait_send()

            @pl.when(in_middle)
            def _():
                l_copy(b, split).wait_send()

    @pl.when(in_middle)
    def _():
        for k in range(1, nb):
            g_copy(k, upper).wait_send()

    for h in range(2):
        for k in range(1, nu):
            f_copy(k, h, sub).wait_send()


def shards(
    nb, ns, nu,
    attention_output_rows,
    residual,
    output_projection_weight,
    down_adapter_bank,
    up_adapter_bank,
    rollout_row_tenant,
    tenant_bank_entry,
    tenant_live_rank,
):
    rows, feats = attention_output_rows.shape
    own, cols = residual.shape
    banks, rank, _ = down_adapter_bank.shape
    up_banks = up_adapter_bank.shape[0]
    total = rollout_row_tenant.shape[0]
    wide = nb // 2 * banks * rank
    fc = PIECE
    per = own // rows
    pieces = feats // nu // fc
    items = (nb - 1) * pieces
    share = rows // nu
    dma = pltpu.SemaphoreType.DMA
    bf16 = jnp.bfloat16
    any_spec = pl.BlockSpec(memory_space=pltpu.HBM)
    vmem = pl.BlockSpec(memory_space=pltpu.VMEM)
    return pl.pallas_call(
        functools.partial(kernel, nb, ns, nu, fc),
        out_shape=pltpu.VMEM((own, cols), bf16),
        in_specs=[any_spec] * 8,
        out_specs=vmem,
        scratch_shapes=[
            pltpu.SMEM(tenant_bank_entry.shape, jnp.int32),
            pltpu.SMEM(tenant_live_rank.shape, jnp.int32),
            pltpu.VMEM((1, total), jnp.int32),
            pltpu.VMEM((rows, feats), bf16),
            pltpu.VMEM((nb, nu, pieces, rows, fc), bf16),
            pltpu.VMEM((feats, cols), bf16),
            pltpu.VMEM((own, cols), bf16),
            pltpu.VMEM((wide, feats), bf16),
            pltpu.VMEM((2 * wide, cols), bf16),
            pltpu.VMEM((total, wide), F32),
            pltpu.VMEM((nb, rows, cols), F32),
            pltpu.VMEM((nb, rows, cols), bf16),
            pltpu.VMEM((ns, per, rows, cols), bf16),
            pltpu.VMEM((per, share, wide), F32),
            pltpu.VMEM((nb, share, wide), F32),
            pltpu.VMEM((ns, per, share, wide), F32),
            pltpu.VMEM((2, nu, share, per * rank), bf16),
            pltpu.VMEM((own, 2 * wide), bf16),
            dma((2,)),
            dma((W_CHUNKS,)),
            dma((banks,)),
            pltpu.SemaphoreType.REGULAR,
            pltpu.SemaphoreType.REGULAR,
            dma((2, RING)),
            dma((items,)),
            dma((nu - 1, 2, 2)),
            dma((nu - 1, 2, 4)),
            dma((ns - 1, up_banks)),
            dma((ns - 1, up_banks)),
            dma((banks,)),
            dma((nb // 2, banks)),
            dma((nu - 1, nb // 2, banks)),
            dma((nu - 1, nb // 2, banks)),
            dma((nb,)),
            dma((ns - 1, per)),
            dma((nb,)),
            dma((ns - 1, per)),
            dma((nb - 1,)),
            dma((2,)),
            dma((nu - 1, 2)),
            dma((nu - 1, 2)),
        ],
        compiler_params=pltpu.CompilerParams(
            collective_id=0, has_side_effects=True, vmem_limit_bytes=60 * 2**20
        ),
    )(
        tenant_bank_entry,
        tenant_live_rank,
        attention_output_rows,
        residual,
        output_projection_weight,
        down_adapter_bank,
        up_adapter_bank,
        rollout_row_tenant.reshape(1, total),
    )


def solution(mesh):
    in_specs = (
        P(("groups", "blk"), "split"),
        P(("groups", "split"), ("blk", "sub")),
        P("split", ("blk", "sub")),
        P("blk", None, "split"),
        P("split", None, ("blk", "sub")),
        P("groups"),
        P(),
        P(),
    )
    out_specs = P(("groups", "split"), ("blk", "sub"))
    body = functools.partial(
        shards, mesh.shape["blk"], mesh.shape["split"], mesh.shape["sub"]
    )
    return jax.shard_map(body, mesh=mesh, in_specs=in_specs, out_specs=out_specs, check_vma=False)
```

```python
import functools

import jax
import jax.numpy as jnp
from jax import lax
from jax.experimental import pallas as pl
from jax.experimental.pallas import tpu as pltpu
from jax.sharding import PartitionSpec as P

PIECE = 256
FLIGHT = 4
LEAD = (4, 3)
RING = max(FLIGHT, *LEAD)
W_CHUNKS = 4
EARLY = 2
MESH = pl.DeviceIdType.MESH
F32 = jnp.float32


def kernel(
    nb, ns, nu, fc,
    ent_any, rank_any, x_ref, r_ref, w_ref, dn_ref, up_ref, ten_any, o_ref,
    ent_ref, rank_ref, ten_ref, xown, xall, wv, rv, dnp, upp, mtab, acc, xs, xr, lacc, ls, lr, lowx, hot,
    sem_loc, sem_w, sem_bank, ready, entered, zsend, zrecv, csend, crecv,
    usend, urecv, bsend, brecv, bcsend, bcrecv, psend, precv, lsend, lrecv, gsend, grecv, fsend, frecv,
):
    blk, split, sub = lax.axis_index("blk"), lax.axis_index("split"), lax.axis_index("sub")
    rows, feats = x_ref.shape
    cols = w_ref.shape[1]
    own = r_ref.shape[0]
    banks, rank = dn_ref.shape[0], dn_ref.shape[1]
    up_banks = up_ref.shape[0]
    wide = dnp.shape[0]
    total = ten_ref.shape[1]
    tenants = ent_ref.shape[0]
    per = own // rows
    half = feats // nu
    pieces = half // fc
    share = rows // nu
    group = nb // 2
    upper = blk // group
    middle = group - 1 + upper
    in_middle = blk == middle
    ticks = (nb - 1) * pieces

    barrier = pltpu.get_barrier_semaphore()

    @pl.when(blk < nb - 1)
    def _():
        pl.semaphore_signal(barrier, inc=1, device_id={"blk": blk + 1}, device_id_type=MESH)

    def peers(upper_ones, sem):
        for axis, n, me in (("split", ns, split), ("sub", nu, sub)):
            for k in range(1, n):
                to = me + k if upper_ones else me - k

                @pl.when(to < n if upper_ones else to >= 0)
                def _():
                    pl.semaphore_signal(
                        sem, inc=1, device_id={axis: jnp.clip(to, 0, n - 1)},
                        device_id_type=MESH,
                    )

    peers(True, barrier)
    below = jnp.where(blk > 0, 1, 0) + split + sub

    @pl.when(below > 0)
    def _():
        pl.semaphore_wait(barrier, below)


    def arrivals(side):
        return (nb - 1 - blk if side == 0 else blk) * pieces

    def sends(side):
        if side == 0:
            return jnp.where(blk > 0, nb - blk, 0) * pieces
        return jnp.where(blk < nb - 1, blk + 1, 0) * pieces

    def is_late(side, to):
        near = jnp.clip(to + 1 - 2 * side, 0, nb - 1)
        return (to == (0 if side == 0 else nb - 1)) & (near // per == split)

    def order(side, to, i):
        sign = 1 - 2 * side
        near = to + sign
        late = is_late(side, to)
        body = (nb - 2) * pieces
        lead = LEAD[side]
        first = i < lead
        last = i >= lead + body
        j = i - lead
        b_late = jnp.where(first | last, near, near + sign * (1 + j // pieces))
        q_late = jnp.where(first, i, jnp.where(last, i - body, lax.rem(j + pieces, pieces)))
        b = jnp.where(late, b_late, near + sign * (i // pieces))
        q = jnp.where(late, q_late, lax.rem(i, pieces))
        return jnp.clip(b, 0, nb - 1), jnp.clip(q, 0, pieces - 1)

    def z_copy(side, i, to, mine=False):
        b, q = order(side, to, i)
        dst = xall.at[b, sub, q]
        src = dst
        if mine:
            src = x_ref.at[:, pl.ds(pl.multiple_of(sub * half + q * fc, fc), fc)]
        return pltpu.make_async_remote_copy(
            src_ref=src,
            dst_ref=dst,
            send_sem=zsend.at[side, lax.rem(i, RING)],
            recv_sem=zrecv.at[i if side == 0 else ticks - 1 - i],
            device_id={"blk": jnp.where(to == blk, lax.rem(blk + 1, nb), jnp.clip(to, 0, nb - 1))},
            device_id_type=MESH,
        )

    def target(side):
        return blk - 1 if side == 0 else blk + 1

    def flight(side):
        return jnp.where(is_late(side, target(side)), LEAD[side], FLIGHT)

    def send(side, i):
        to = target(side)
        b, _ = order(side, to, i)

        @pl.when((i < sends(side)) & (b == blk))
        def _():
            z_copy(side, i, to, True).start()

        @pl.when((i < sends(side)) & (b != blk))
        def _():
            z_copy(side, i, to).start()

    def c_copy(side, i, k, core):
        b, q = order(side, blk, i)
        piece = xall.at[b, core, q]
        return pltpu.make_async_remote_copy(
            src_ref=piece,
            dst_ref=piece,
            send_sem=csend.at[k - 1, side, lax.rem(i, 2)],
            recv_sem=crecv.at[k - 1, side, lax.rem(i, 4)],
            device_id={"sub": lax.rem(sub + k, nu)},
            device_id_type=MESH,
        )

    x_load = pltpu.make_async_copy(x_ref, xown, sem_loc.at[0])
    wrows = feats // W_CHUNKS
    w_loads = [
        pltpu.make_async_copy(
            w_ref.at[pl.ds(n * wrows, wrows)], wv.at[pl.ds(n * wrows, wrows)], sem_w.at[n]
        )
        for n in range(W_CHUNKS)
    ]

    @pl.when(blk > 0)
    def _():
        pl.semaphore_signal(ready, inc=1, device_id={"blk": blk - 1}, device_id_type=MESH)

    for i in range(RING):
        @pl.when(i < flight(0))
        def _():
            send(0, i)

    peers(False, entered)

    x_load.start()
    for load in w_loads:
        load.start()

    above = ns + nu - 2 - split - sub

    @pl.when(above > 0)
    def _():
        pl.semaphore_wait(entered, above)

    @pl.when(blk < nb - 1)
    def _():
        pl.semaphore_wait(ready, 1)

    for i in range(RING):
        @pl.when(i < flight(1))
        def _():
            send(1, i)

    r_load = pltpu.make_async_copy(r_ref, rv, sem_loc.at[1])
    r_load.start()

    def bank_slot(place, e):
        return dnp.at[pl.ds(pl.multiple_of((place * banks + e) * rank, rank), rank)]

    table_loads = [
        pltpu.make_async_copy(src, dst, sem_loc.at[1])
        for src, dst in ((ent_any, ent_ref), (rank_any, rank_ref), (ten_any, ten_ref))
    ]
    bank_loads = [
        pltpu.make_async_copy(dn_ref.at[e], bank_slot(blk % group, e), sem_bank.at[e])
        for e in range(banks)
    ]

    @pl.when(in_middle)
    def _():
        for load in bank_loads:
            load.start()

    for load in table_loads:
        load.start()

    def up_slot(bank):
        return upp.at[pl.ds(pl.multiple_of(bank * rank, rank), rank)]

    up_loads = [
        pltpu.make_async_copy(up_ref.at[e], up_slot(split * up_banks + e), sem_loc.at[1])
        for e in range(up_banks)
    ]
    for load in up_loads:
        load.start()

    def u_copy(k, e, owner):
        return pltpu.make_async_remote_copy(
            src_ref=up_ref.at[e],
            dst_ref=up_slot(owner * up_banks + e),
            send_sem=usend.at[k - 1, e],
            recv_sem=urecv.at[k - 1, e],
            device_id={"split": lax.rem(split + k, ns)},
            device_id_type=MESH,
        )

    for k in range(1, ns):
        for e in range(up_banks):
            u_copy(k, e, split).start()

    half_lanes = pl.ds(pl.multiple_of(sub * half, half), half)

    def bank_half(place, e, core):
        return dnp.at[
            pl.ds(pl.multiple_of((place * banks + e) * rank, rank), rank),
            pl.ds(pl.multiple_of(core * half, half), half),
        ]

    def b_copy(e, place):
        return pltpu.make_async_remote_copy(
            src_ref=dn_ref.at[e, :, half_lanes],
            dst_ref=bank_half(place, e, sub),
            send_sem=bsend.at[e],
            recv_sem=brecv.at[place, e],
            device_id={"blk": middle},
            device_id_type=MESH,
        )

    def bc_copy(e, place, k, core):
        return pltpu.make_async_remote_copy(
            src_ref=bank_half(place, e, core),
            dst_ref=bank_half(place, e, core),
            send_sem=bcsend.at[k - 1, place, e],
            recv_sem=bcrecv.at[k - 1, place, e],
            device_id={"sub": lax.rem(sub + k, nu)},
            device_id_type=MESH,
        )

    def p_copy(b, src):
        owner = b // per
        return pltpu.make_async_remote_copy(
            src_ref=xs.at[b],
            dst_ref=xr.at[src, b - owner * per],
            send_sem=psend.at[b],
            recv_sem=precv.at[lax.rem(src - owner + ns, ns) - 1, b - owner * per],
            device_id={"split": owner},
            device_id_type=MESH,
        )

    def l_copy(b, src):
        owner = b // per
        return pltpu.make_async_remote_copy(
            src_ref=ls.at[b],
            dst_ref=lr.at[src, b - owner * per],
            send_sem=lsend.at[b],
            recv_sem=lrecv.at[lax.rem(src - owner + ns, ns) - 1, b - owner * per],
            device_id={"split": owner},
            device_id_type=MESH,
        )

    def g_copy(k, h):
        return pltpu.make_async_remote_copy(
            src_ref=lowx.at[h, sub],
            dst_ref=lowx.at[h, sub],
            send_sem=gsend.at[k - 1],
            recv_sem=grecv.at[h],
            device_id={"blk": lax.rem(blk + k, nb)},
            device_id_type=MESH,
        )

    def f_copy(k, h, core):
        return pltpu.make_async_remote_copy(
            src_ref=lowx.at[h, core],
            dst_ref=lowx.at[h, core],
            send_sem=fsend.at[k - 1, h],
            recv_sem=frecv.at[k - 1, h],
            device_id={"sub": lax.rem(sub + k, nu)},
            device_id_type=MESH,
        )

    def columns(tens):
        n = tens.shape[1]
        return jnp.transpose(jnp.broadcast_to(tens.astype(F32), (8, n)))[:, :1]

    def make_tables():
        for load in table_loads + up_loads + [r_load]:
            load.wait()
        lanes = lax.broadcasted_iota(jnp.int32, (1, 2 * wide), 1)
        tcol = columns(ten_ref[:, pl.ds(pl.multiple_of(split * own, own), own)])
        table = jnp.zeros((own, 2 * wide), F32)
        for t in range(tenants):
            first = jnp.full((1, 2 * wide), ent_ref[t], jnp.int32) * rank
            line = jnp.where((lanes >= first) & (lanes < first + rank), 1.0, 0.0)
            table = jnp.where(tcol == t, line, table)
        hot[...] = table.astype(hot.dtype)

        @pl.when(in_middle)
        def _():
            lane = lax.broadcasted_iota(jnp.int32, (1, wide), 1)
            tcol = columns(ten_ref[...])
            table = jnp.zeros((total, wide), F32)
            for t in range(tenants):
                live = jnp.full((1, wide), rank_ref[t], jnp.int32)
                slot = jnp.full((1, wide), ent_ref[t], jnp.int32)
                line = jnp.zeros((1, wide), F32)
                for e in range(group * banks):
                    keep = (
                        (lane >= e * rank) & (lane < e * rank + jnp.minimum(live, rank))
                        & (slot == upper * group * banks + e)
                    )
                    line = jnp.where(keep, rank / live.astype(F32), line)
                table = jnp.where(tcol == t, line, table)
            mtab[...] = table

    def finish(b):
        @pl.when(b // per != split)
        def _():
            xs[b] = acc[b].astype(xs.dtype)
            p_copy(b, split).start()

    def own_rows(n):
        if n == 0:
            x_load.wait()
        for m in range(W_CHUNKS):
            if min(m, 2) == n:
                w_loads[m].wait()
        here = slice(n * wrows, (n + 1) * wrows)
        part = jnp.dot(xown[:, here], wv[here, :], preferred_element_type=F32)
        if n == 0:
            acc[blk] = part
        else:
            acc[blk] += part
        if n == W_CHUNKS - 1:
            finish(blk)

    def own_pieces():
        for c in range(nu):
            for q in range(pieces):
                xall[blk, c, q] = xown[:, c * half + q * fc:c * half + (q + 1) * fc]

    def gather(side, i):
        @pl.when((i >= 0) & (i < arrivals(side)))
        def _():
            for k in range(1, nu):
                c_copy(side, i, k, lax.rem(sub - k + nu, nu)).wait_recv()
                c_copy(side, i, k, sub).wait_send()

    def compute(side, i):
        @pl.when((i >= 0) & (i < arrivals(side)))
        def _():
            b, q = order(side, blk, i)
            part = jnp.zeros((rows, cols), F32)
            for c in range(nu):
                at = pl.ds(pl.multiple_of(c * half + q * fc, fc), fc)
                part = part + jnp.dot(xall[b, c, q], wv[at, :], preferred_element_type=F32)

            @pl.when(q == 0)
            def _():
                acc[b] = part

            @pl.when(q != 0)
            def _():
                acc[b] += part

            @pl.when(q == pieces - 1)
            def _():
                finish(b)

    def each_far_bank(body):
        for p in range(group):
            @pl.when(p != blk % group)
            def _():
                for e in range(banks):
                    body(e, p)

    def banks_in():
        for load in bank_loads:
            load.wait()

        def body(e, p):
            b_copy(e, p).wait_recv()
            for k in range(1, nu):
                bc_copy(e, p, k, sub).start()

        each_far_bank(body)

    def banks_shared():
        def body(e, p):
            for k in range(1, nu):
                bc_copy(e, p, k, lax.rem(sub - k + nu, nu)).wait_recv()
                bc_copy(e, p, k, sub).wait_send()

        each_far_bank(body)

    def low_work(blocks):
        part_rows = pl.ds(pl.multiple_of(sub * share, share), share)
        low = jnp.zeros((len(blocks) * share, wide), F32)
        for c in range(nu):
            for q in range(pieces):
                x = jnp.concatenate([xall[b, c, q, part_rows, :] for b in blocks], axis=0)
                d = dnp[:, c * half + q * fc:c * half + (q + 1) * fc]
                low = low + lax.dot_general(
                    x, d, (((1,), (1,)), ((), ())), preferred_element_type=F32
                )
        for m, b in enumerate(blocks):
            mine = low[m * share:(m + 1) * share]

            @pl.when(b // per == split)
            def _():
                lacc[b - split * per] = mine

            @pl.when(b // per != split)
            def _():
                ls[b] = mine
                l_copy(b, split).start()

    def low_early():
        some = 3 if (nb - 1) % 3 == 0 else 1

        @pl.loop(0, (nb - 1) // some)
        def _(n):
            low_work([n * some + m + upper for m in range(some)])

    def low_spread():
        kept = []
        for o in range(per):
            b = split * per + o
            low = lacc[o]
            for k in range(1, ns):
                src = lax.rem(split + k, ns)
                l_copy(b, src).wait_recv()
                low = low + lr[src, o]
            low = low * mtab[pl.ds(pl.multiple_of(b * rows + sub * share, share), share), :]
            kept.append(
                sum(low[:, e * rank:(e + 1) * rank] for e in range(1, wide // rank))
                + low[:, :rank]
            )
        lowx[upper, sub] = jnp.concatenate(kept, axis=1).astype(lowx.dtype)
        for k in range(1, nb):
            g_copy(k, upper).start()

    def low_share():
        for h in range(2):
            @pl.when(jnp.logical_not(in_middle & (upper == h)))
            def _():
                g_copy(1, h).wait_recv()
            for k in range(1, nu):
                f_copy(k, h, sub).start()

    low_tick = group * pieces + 1
    away = jnp.where(upper == 0, middle - blk, blk - middle)
    bank_tick = jnp.maximum(pieces - FLIGHT + 1, (away - 1) * pieces + 1)

    def low_use():
        for k in range(1, ns):
            for e in range(up_banks):
                u_copy(k, e, lax.rem(split - k + ns, ns)).wait_recv()
        for h in range(2):
            for k in range(1, nu):
                f_copy(k, h, lax.rem(sub - k + nu, nu)).wait_recv()
        low = jnp.concatenate([lowx[0, c] + lowx[1, c] for c in range(nu)], axis=0)
        for o in range(per):
            here = slice(o * rows, (o + 1) * rows)
            low_o = low[:, o * rank:(o + 1) * rank]
            low_o = jnp.concatenate([low_o] * (2 * wide // rank), axis=1) * hot[here, :]
            acc[split * per + o] += rv[here, :].astype(F32) + jnp.dot(
                low_o, upp[...], preferred_element_type=F32
            )

    def arrive(side, i):
        @pl.when((i >= 0) & (i < arrivals(side)))
        def _():
            z_copy(side, i, blk).wait_recv()
            for k in range(1, nu):
                c_copy(side, i, k, sub).start()

    @pl.loop(0, ticks + 2)
    def _(t):
        @pl.when((t == low_tick + 1) & in_middle)
        def _():
            low_spread()

        for side in range(2):
            arrive(side, t - 1)

            @pl.when((t >= 1) & (t - 1 + flight(side) < sends(side)))
            def _():
                z_copy(side, t - 1, target(side)).wait_send()
                send(side, t - 1 + flight(side))

        @pl.when((t == bank_tick) & jnp.logical_not(in_middle))
        def _():
            for e in range(banks):
                b_copy(e, blk % group).start()

        for n in range(W_CHUNKS):
            @pl.when(t == n)
            def _():
                own_rows(n)

        @pl.when(t == W_CHUNKS)
        def _():
            make_tables()

        @pl.when((t == W_CHUNKS + 1) & in_middle)
        def _():
            own_pieces()

        @pl.when((t == low_tick - 4) & in_middle)
        def _():
            banks_in()

        @pl.when((t == low_tick - 3) & in_middle)
        def _():
            banks_shared()

        @pl.when(t == ticks - 1)
        def _():
            low_share()

        @pl.when(t == ticks)
        def _():
            low_use()

        for side in range(2):
            gather(side, t - 2)

        @pl.when((t == low_tick) & in_middle)
        def _():
            low_work([jnp.where(upper == 0, nb - 1, 0)])

        for side in range(2):
            compute(side, t - 2)

        @pl.when((t == low_tick - EARLY) & in_middle)
        def _():
            low_early()

    for o in range(per):
        b = split * per + o
        value = acc[b]
        for k in range(1, ns):
            src = lax.rem(split + k, ns)
            p_copy(b, src).wait_recv()
            value = value + xr[src, o].astype(F32)
        o_ref[o * rows:(o + 1) * rows, :] = value.astype(o_ref.dtype)

    for side in range(2):
        for n in range(RING):
            @pl.when((sends(side) > 0) & (n < flight(side)))
            def _():
                z_copy(side, sends(side) - 1 - n, target(side)).wait_send()
    for k in range(1, ns):
        for e in range(up_banks):
            u_copy(k, e, split).wait_send()

    @pl.when(jnp.logical_not(in_middle))
    def _():
        for e in range(banks):
            b_copy(e, blk % group).wait_send()

    for b in range(nb):
        @pl.when(b // per != split)
        def _():
            p_copy(b, split).wait_send()

            @pl.when(in_middle)
            def _():
                l_copy(b, split).wait_send()

    @pl.when(in_middle)
    def _():
        for k in range(1, nb):
            g_copy(k, upper).wait_send()

    for h in range(2):
        for k in range(1, nu):
            f_copy(k, h, sub).wait_send()


def shards(
    nb, ns, nu,
    attention_output_rows,
    residual,
    output_projection_weight,
    down_adapter_bank,
    up_adapter_bank,
    rollout_row_tenant,
    tenant_bank_entry,
    tenant_live_rank,
):
    rows, feats = attention_output_rows.shape
    own, cols = residual.shape
    banks, rank, _ = down_adapter_bank.shape
    up_banks = up_adapter_bank.shape[0]
    total = rollout_row_tenant.shape[0]
    wide = nb // 2 * banks * rank
    fc = PIECE
    per = own // rows
    pieces = feats // nu // fc
    items = (nb - 1) * pieces
    share = rows // nu
    dma = pltpu.SemaphoreType.DMA
    bf16 = jnp.bfloat16
    any_spec = pl.BlockSpec(memory_space=pltpu.HBM)
    vmem = pl.BlockSpec(memory_space=pltpu.VMEM)
    return pl.pallas_call(
        functools.partial(kernel, nb, ns, nu, fc),
        out_shape=pltpu.VMEM((own, cols), bf16),
        in_specs=[any_spec] * 8,
        out_specs=vmem,
        scratch_shapes=[
            pltpu.SMEM(tenant_bank_entry.shape, jnp.int32),
            pltpu.SMEM(tenant_live_rank.shape, jnp.int32),
            pltpu.VMEM((1, total), jnp.int32),
            pltpu.VMEM((rows, feats), bf16),
            pltpu.VMEM((nb, nu, pieces, rows, fc), bf16),
            pltpu.VMEM((feats, cols), bf16),
            pltpu.VMEM((own, cols), bf16),
            pltpu.VMEM((wide, feats), bf16),
            pltpu.VMEM((2 * wide, cols), bf16),
            pltpu.VMEM((total, wide), F32),
            pltpu.VMEM((nb, rows, cols), F32),
            pltpu.VMEM((nb, rows, cols), bf16),
            pltpu.VMEM((ns, per, rows, cols), bf16),
            pltpu.VMEM((per, share, wide), F32),
            pltpu.VMEM((nb, share, wide), F32),
            pltpu.VMEM((ns, per, share, wide), F32),
            pltpu.VMEM((2, nu, share, per * rank), bf16),
            pltpu.VMEM((own, 2 * wide), bf16),
            dma((2,)),
            dma((W_CHUNKS,)),
            dma((banks,)),
            pltpu.SemaphoreType.REGULAR,
            pltpu.SemaphoreType.REGULAR,
            dma((2, RING)),
            dma((items,)),
            dma((nu - 1, 2, 2)),
            dma((nu - 1, 2, 4)),
            dma((ns - 1, up_banks)),
            dma((ns - 1, up_banks)),
            dma((banks,)),
            dma((nb // 2, banks)),
            dma((nu - 1, nb // 2, banks)),
            dma((nu - 1, nb // 2, banks)),
            dma((nb,)),
            dma((ns - 1, per)),
            dma((nb,)),
            dma((ns - 1, per)),
            dma((nb - 1,)),
            dma((2,)),
            dma((nu - 1, 2)),
            dma((nu - 1, 2)),
        ],
        compiler_params=pltpu.CompilerParams(
            collective_id=0, has_side_effects=True, vmem_limit_bytes=60 * 2**20
        ),
    )(
        tenant_bank_entry,
        tenant_live_rank,
        attention_output_rows,
        residual,
        output_projection_weight,
        down_adapter_bank,
        up_adapter_bank,
        rollout_row_tenant.reshape(1, total),
    )


def solution(mesh):
    in_specs = (
        P(("groups", "blk"), "split"),
        P(("groups", "split"), ("blk", "sub")),
        P("split", ("blk", "sub")),
        P("blk", None, "split"),
        P("split", None, ("blk", "sub")),
        P("groups"),
        P(),
        P(),
    )
    out_specs = P(("groups", "split"), ("blk", "sub"))
    body = functools.partial(
        shards, mesh.shape["blk"], mesh.shape["split"], mesh.shape["sub"]
    )
    return jax.shard_map(body, mesh=mesh, in_specs=in_specs, out_specs=out_specs, check_vma=False)
```

```python
import functools

import jax
import jax.numpy as jnp
from jax import lax
from jax.experimental import pallas as pl
from jax.experimental.pallas import tpu as pltpu
from jax.sharding import PartitionSpec as P

PIECE = 256
FLIGHT = 4
LEAD = (4, 3)
RING = max(FLIGHT, *LEAD)
W_CHUNKS = 4
EARLY = 3
MESH = pl.DeviceIdType.MESH
F32 = jnp.float32


def kernel(
    nb, ns, nu, fc,
    ent_any, rank_any, x_ref, r_ref, w_ref, dn_ref, up_ref, ten_any, o_ref,
    ent_ref, rank_ref, ten_ref, xown, xall, wv, rv, dnp, upp, mtab, acc, xs, xr, lacc, ls, lr, lowx, hot,
    sem_loc, sem_w, sem_bank, ready, entered, zsend, zrecv, csend, crecv,
    usend, urecv, bsend, brecv, bcsend, bcrecv, psend, precv, lsend, lrecv, gsend, grecv, fsend, frecv,
):
    blk, split, sub = lax.axis_index("blk"), lax.axis_index("split"), lax.axis_index("sub")
    rows, feats = x_ref.shape
    cols = w_ref.shape[1]
    own = r_ref.shape[0]
    banks, rank = dn_ref.shape[0], dn_ref.shape[1]
    up_banks = up_ref.shape[0]
    wide = dnp.shape[0]
    total = ten_ref.shape[1]
    tenants = ent_ref.shape[0]
    per = own // rows
    half = feats // nu
    pieces = half // fc
    share = rows // nu
    group = nb // 2
    upper = blk // group
    middle = group - 1 + upper
    in_middle = blk == middle
    ticks = (nb - 1) * pieces

    barrier = pltpu.get_barrier_semaphore()

    @pl.when(blk < nb - 1)
    def _():
        pl.semaphore_signal(barrier, inc=1, device_id={"blk": blk + 1}, device_id_type=MESH)

    def peers(upper_ones, sem):
        for axis, n, me in (("split", ns, split), ("sub", nu, sub)):
            for k in range(1, n):
                to = me + k if upper_ones else me - k

                @pl.when(to < n if upper_ones else to >= 0)
                def _():
                    pl.semaphore_signal(
                        sem, inc=1, device_id={axis: jnp.clip(to, 0, n - 1)},
                        device_id_type=MESH,
                    )

    peers(True, barrier)
    below = jnp.where(blk > 0, 1, 0) + split + sub

    @pl.when(below > 0)
    def _():
        pl.semaphore_wait(barrier, below)


    def arrivals(side):
        return (nb - 1 - blk if side == 0 else blk) * pieces

    def sends(side):
        if side == 0:
            return jnp.where(blk > 0, nb - blk, 0) * pieces
        return jnp.where(blk < nb - 1, blk + 1, 0) * pieces

    def is_late(side, to):
        near = jnp.clip(to + 1 - 2 * side, 0, nb - 1)
        return (to == (0 if side == 0 else nb - 1)) & (near // per == split)

    def order(side, to, i):
        sign = 1 - 2 * side
        near = to + sign
        late = is_late(side, to)
        body = (nb - 2) * pieces
        lead = LEAD[side]
        first = i < lead
        last = i >= lead + body
        j = i - lead
        b_late = jnp.where(first | last, near, near + sign * (1 + j // pieces))
        q_late = jnp.where(first, i, jnp.where(last, i - body, lax.rem(j + pieces, pieces)))
        b = jnp.where(late, b_late, near + sign * (i // pieces))
        q = jnp.where(late, q_late, lax.rem(i, pieces))
        return jnp.clip(b, 0, nb - 1), jnp.clip(q, 0, pieces - 1)

    def z_copy(side, i, to, mine=False):
        b, q = order(side, to, i)
        dst = xall.at[b, sub, q]
        src = dst
        if mine:
            src = x_ref.at[:, pl.ds(pl.multiple_of(sub * half + q * fc, fc), fc)]
        return pltpu.make_async_remote_copy(
            src_ref=src,
            dst_ref=dst,
            send_sem=zsend.at[side, lax.rem(i, RING)],
            recv_sem=zrecv.at[i if side == 0 else ticks - 1 - i],
            device_id={"blk": jnp.where(to == blk, lax.rem(blk + 1, nb), jnp.clip(to, 0, nb - 1))},
            device_id_type=MESH,
        )

    def target(side):
        return blk - 1 if side == 0 else blk + 1

    def flight(side):
        return jnp.where(is_late(side, target(side)), LEAD[side], FLIGHT)

    def send(side, i):
        to = target(side)
        b, _ = order(side, to, i)

        @pl.when((i < sends(side)) & (b == blk))
        def _():
            z_copy(side, i, to, True).start()

        @pl.when((i < sends(side)) & (b != blk))
        def _():
            z_copy(side, i, to).start()

    def c_copy(side, i, k, core):
        b, q = order(side, blk, i)
        piece = xall.at[b, core, q]
        return pltpu.make_async_remote_copy(
            src_ref=piece,
            dst_ref=piece,
            send_sem=csend.at[k - 1, side, lax.rem(i, 2)],
            recv_sem=crecv.at[k - 1, side, lax.rem(i, 4)],
            device_id={"sub": lax.rem(sub + k, nu)},
            device_id_type=MESH,
        )

    x_load = pltpu.make_async_copy(x_ref, xown, sem_loc.at[0])
    wrows = feats // W_CHUNKS
    w_loads = [
        pltpu.make_async_copy(
            w_ref.at[pl.ds(n * wrows, wrows)], wv.at[pl.ds(n * wrows, wrows)], sem_w.at[n]
        )
        for n in range(W_CHUNKS)
    ]

    @pl.when(blk > 0)
    def _():
        pl.semaphore_signal(ready, inc=1, device_id={"blk": blk - 1}, device_id_type=MESH)

    for i in range(RING):
        @pl.when(i < flight(0))
        def _():
            send(0, i)

    peers(False, entered)

    x_load.start()
    for load in w_loads:
        load.start()

    above = ns + nu - 2 - split - sub

    @pl.when(above > 0)
    def _():
        pl.semaphore_wait(entered, above)

    @pl.when(blk < nb - 1)
    def _():
        pl.semaphore_wait(ready, 1)

    for i in range(RING):
        @pl.when(i < flight(1))
        def _():
            send(1, i)

    r_load = pltpu.make_async_copy(r_ref, rv, sem_loc.at[1])
    r_load.start()

    def bank_slot(place, e):
        return dnp.at[pl.ds(pl.multiple_of((place * banks + e) * rank, rank), rank)]

    table_loads = [
        pltpu.make_async_copy(src, dst, sem_loc.at[1])
        for src, dst in ((ent_any, ent_ref), (rank_any, rank_ref), (ten_any, ten_ref))
    ]
    bank_loads = [
        pltpu.make_async_copy(dn_ref.at[e], bank_slot(blk % group, e), sem_bank.at[e])
        for e in range(banks)
    ]

    @pl.when(in_middle)
    def _():
        for load in bank_loads:
            load.start()

    for load in table_loads:
        load.start()

    def up_slot(bank):
        return upp.at[pl.ds(pl.multiple_of(bank * rank, rank), rank)]

    up_loads = [
        pltpu.make_async_copy(up_ref.at[e], up_slot(split * up_banks + e), sem_loc.at[1])
        for e in range(up_banks)
    ]
    for load in up_loads:
        load.start()

    def u_copy(k, e, owner):
        return pltpu.make_async_remote_copy(
            src_ref=up_ref.at[e],
            dst_ref=up_slot(owner * up_banks + e),
            send_sem=usend.at[k - 1, e],
            recv_sem=urecv.at[k - 1, e],
            device_id={"split": lax.rem(split + k, ns)},
            device_id_type=MESH,
        )

    for k in range(1, ns):
        for e in range(up_banks):
            u_copy(k, e, split).start()

    half_lanes = pl.ds(pl.multiple_of(sub * half, half), half)

    def bank_half(place, e, core):
        return dnp.at[
            pl.ds(pl.multiple_of((place * banks + e) * rank, rank), rank),
            pl.ds(pl.multiple_of(core * half, half), half),
        ]

    def b_copy(e, place):
        return pltpu.make_async_remote_copy(
            src_ref=dn_ref.at[e, :, half_lanes],
            dst_ref=bank_half(place, e, sub),
            send_sem=bsend.at[e],
            recv_sem=brecv.at[place, e],
            device_id={"blk": middle},
            device_id_type=MESH,
        )

    def bc_copy(e, place, k, core):
        return pltpu.make_async_remote_copy(
            src_ref=bank_half(place, e, core),
            dst_ref=bank_half(place, e, core),
            send_sem=bcsend.at[k - 1, place, e],
            recv_sem=bcrecv.at[k - 1, place, e],
            device_id={"sub": lax.rem(sub + k, nu)},
            device_id_type=MESH,
        )

    def p_copy(b, src):
        owner = b // per
        return pltpu.make_async_remote_copy(
            src_ref=xs.at[b],
            dst_ref=xr.at[src, b - owner * per],
            send_sem=psend.at[b],
            recv_sem=precv.at[lax.rem(src - owner + ns, ns) - 1, b - owner * per],
            device_id={"split": owner},
            device_id_type=MESH,
        )

    def l_copy(b, src):
        owner = b // per
        return pltpu.make_async_remote_copy(
            src_ref=ls.at[b],
            dst_ref=lr.at[src, b - owner * per],
            send_sem=lsend.at[b],
            recv_sem=lrecv.at[lax.rem(src - owner + ns, ns) - 1, b - owner * per],
            device_id={"split": owner},
            device_id_type=MESH,
        )

    def g_copy(k, h):
        return pltpu.make_async_remote_copy(
            src_ref=lowx.at[h, sub],
            dst_ref=lowx.at[h, sub],
            send_sem=gsend.at[k - 1],
            recv_sem=grecv.at[h],
            device_id={"blk": lax.rem(blk + k, nb)},
            device_id_type=MESH,
        )

    def f_copy(k, h, core):
        return pltpu.make_async_remote_copy(
            src_ref=lowx.at[h, core],
            dst_ref=lowx.at[h, core],
            send_sem=fsend.at[k - 1, h],
            recv_sem=frecv.at[k - 1, h],
            device_id={"sub": lax.rem(sub + k, nu)},
            device_id_type=MESH,
        )

    def columns(tens):
        n = tens.shape[1]
        return jnp.transpose(jnp.broadcast_to(tens.astype(F32), (8, n)))[:, :1]

    def make_tables():
        for load in table_loads + up_loads + [r_load]:
            load.wait()
        lanes = lax.broadcasted_iota(jnp.int32, (1, 2 * wide), 1)
        tcol = columns(ten_ref[:, pl.ds(pl.multiple_of(split * own, own), own)])
        table = jnp.zeros((own, 2 * wide), F32)
        for t in range(tenants):
            first = jnp.full((1, 2 * wide), ent_ref[t], jnp.int32) * rank
            line = jnp.where((lanes >= first) & (lanes < first + rank), 1.0, 0.0)
            table = jnp.where(tcol == t, line, table)
        hot[...] = table.astype(hot.dtype)

        @pl.when(in_middle)
        def _():
            lane = lax.broadcasted_iota(jnp.int32, (1, wide), 1)
            tcol = columns(ten_ref[...])
            table = jnp.zeros((total, wide), F32)
            for t in range(tenants):
                live = jnp.full((1, wide), rank_ref[t], jnp.int32)
                slot = jnp.full((1, wide), ent_ref[t], jnp.int32)
                line = jnp.zeros((1, wide), F32)
                for e in range(group * banks):
                    keep = (
                        (lane >= e * rank) & (lane < e * rank + jnp.minimum(live, rank))
                        & (slot == upper * group * banks + e)
                    )
                    line = jnp.where(keep, rank / live.astype(F32), line)
                table = jnp.where(tcol == t, line, table)
            mtab[...] = table

    def finish(b):
        @pl.when(b // per != split)
        def _():
            xs[b] = acc[b].astype(xs.dtype)
            p_copy(b, split).start()

    def own_rows(n):
        if n == 0:
            x_load.wait()
        for m in range(W_CHUNKS):
            if min(m, 2) == n:
                w_loads[m].wait()
        here = slice(n * wrows, (n + 1) * wrows)
        part = jnp.dot(xown[:, here], wv[here, :], preferred_element_type=F32)
        if n == 0:
            acc[blk] = part
        else:
            acc[blk] += part
        if n == W_CHUNKS - 1:
            finish(blk)

    def own_pieces():
        for c in range(nu):
            for q in range(pieces):
                xall[blk, c, q] = xown[:, c * half + q * fc:c * half + (q + 1) * fc]

    def gather(side, i):
        @pl.when((i >= 0) & (i < arrivals(side)))
        def _():
            for k in range(1, nu):
                c_copy(side, i, k, lax.rem(sub - k + nu, nu)).wait_recv()
                c_copy(side, i, k, sub).wait_send()

    def compute(side, i):
        @pl.when((i >= 0) & (i < arrivals(side)))
        def _():
            b, q = order(side, blk, i)
            part = jnp.zeros((rows, cols), F32)
            for c in range(nu):
                at = pl.ds(pl.multiple_of(c * half + q * fc, fc), fc)
                part = part + jnp.dot(xall[b, c, q], wv[at, :], preferred_element_type=F32)

            @pl.when(q == 0)
            def _():
                acc[b] = part

            @pl.when(q != 0)
            def _():
                acc[b] += part

            @pl.when(q == pieces - 1)
            def _():
                finish(b)

    def each_far_bank(body):
        for p in range(group):
            @pl.when(p != blk % group)
            def _():
                for e in range(banks):
                    body(e, p)

    def banks_in():
        for load in bank_loads:
            load.wait()

        def body(e, p):
            b_copy(e, p).wait_recv()
            for k in range(1, nu):
                bc_copy(e, p, k, sub).start()

        each_far_bank(body)

    def banks_shared():
        def body(e, p):
            for k in range(1, nu):
                bc_copy(e, p, k, lax.rem(sub - k + nu, nu)).wait_recv()
                bc_copy(e, p, k, sub).wait_send()

        each_far_bank(body)

    def low_work(blocks):
        part_rows = pl.ds(pl.multiple_of(sub * share, share), share)
        low = jnp.zeros((len(blocks) * share, wide), F32)
        for c in range(nu):
            for q in range(pieces):
                x = jnp.concatenate([xall[b, c, q, part_rows, :] for b in blocks], axis=0)
                d = dnp[:, c * half + q * fc:c * half + (q + 1) * fc]
                low = low + lax.dot_general(
                    x, d, (((1,), (1,)), ((), ())), preferred_element_type=F32
                )
        for m, b in enumerate(blocks):
            mine = low[m * share:(m + 1) * share]

            @pl.when(b // per == split)
            def _():
                lacc[b - split * per] = mine

            @pl.when(b // per != split)
            def _():
                ls[b] = mine
                l_copy(b, split).start()

    def low_early():
        some = 3 if (nb - 1) % 3 == 0 else 1

        @pl.loop(0, (nb - 1) // some)
        def _(n):
            low_work([n * some + m + upper for m in range(some)])

    def low_spread():
        kept = []
        for o in range(per):
            b = split * per + o
            low = lacc[o]
            for k in range(1, ns):
                src = lax.rem(split + k, ns)
                l_copy(b, src).wait_recv()
                low = low + lr[src, o]
            low = low * mtab[pl.ds(pl.multiple_of(b * rows + sub * share, share), share), :]
            kept.append(
                sum(low[:, e * rank:(e + 1) * rank] for e in range(1, wide // rank))
                + low[:, :rank]
            )
        lowx[upper, sub] = jnp.concatenate(kept, axis=1).astype(lowx.dtype)
        for k in range(1, nb):
            g_copy(k, upper).start()

    def low_share():
        for h in range(2):
            @pl.when(jnp.logical_not(in_middle & (upper == h)))
            def _():
                g_copy(1, h).wait_recv()
            for k in range(1, nu):
                f_copy(k, h, sub).start()

    low_tick = group * pieces + 1
    away = jnp.where(upper == 0, middle - blk, blk - middle)
    bank_tick = jnp.maximum(pieces - FLIGHT + 1, (away - 1) * pieces + 1)

    def low_use():
        for k in range(1, ns):
            for e in range(up_banks):
                u_copy(k, e, lax.rem(split - k + ns, ns)).wait_recv()
        for h in range(2):
            for k in range(1, nu):
                f_copy(k, h, lax.rem(sub - k + nu, nu)).wait_recv()
        low = jnp.concatenate([lowx[0, c] + lowx[1, c] for c in range(nu)], axis=0)
        for o in range(per):
            here = slice(o * rows, (o + 1) * rows)
            low_o = low[:, o * rank:(o + 1) * rank]
            low_o = jnp.concatenate([low_o] * (2 * wide // rank), axis=1) * hot[here, :]
            acc[split * per + o] += rv[here, :].astype(F32) + jnp.dot(
                low_o, upp[...], preferred_element_type=F32
            )

    def arrive(side, i):
        @pl.when((i >= 0) & (i < arrivals(side)))
        def _():
            z_copy(side, i, blk).wait_recv()
            for k in range(1, nu):
                c_copy(side, i, k, sub).start()

    @pl.loop(0, ticks + 2)
    def _(t):
        @pl.when((t == low_tick + 1) & in_middle)
        def _():
            low_spread()

        for side in range(2):
            arrive(side, t - 1)

            @pl.when((t >= 1) & (t - 1 + flight(side) < sends(side)))
            def _():
                z_copy(side, t - 1, target(side)).wait_send()
                send(side, t - 1 + flight(side))

        @pl.when((t == bank_tick) & jnp.logical_not(in_middle))
        def _():
            for e in range(banks):
                b_copy(e, blk % group).start()

        for n in range(W_CHUNKS):
            @pl.when(t == n)
            def _():
                own_rows(n)

        @pl.when(t == W_CHUNKS)
        def _():
            make_tables()

        @pl.when((t == W_CHUNKS + 1) & in_middle)
        def _():
            own_pieces()

        @pl.when((t == low_tick - 4) & in_middle)
        def _():
            banks_in()

        @pl.when((t == low_tick - 3) & in_middle)
        def _():
            banks_shared()

        @pl.when(t == ticks - 1)
        def _():
            low_share()

        @pl.when(t == ticks)
        def _():
            low_use()

        for side in range(2):
            gather(side, t - 2)

        @pl.when((t == low_tick) & in_middle)
        def _():
            low_work([jnp.where(upper == 0, nb - 1, 0)])

        for side in range(2):
            compute(side, t - 2)

        @pl.when((t == low_tick - EARLY) & in_middle)
        def _():
            low_early()

    for o in range(per):
        b = split * per + o
        value = acc[b]
        for k in range(1, ns):
            src = lax.rem(split + k, ns)
            p_copy(b, src).wait_recv()
            value = value + xr[src, o].astype(F32)
        o_ref[o * rows:(o + 1) * rows, :] = value.astype(o_ref.dtype)

    for side in range(2):
        for n in range(RING):
            @pl.when((sends(side) > 0) & (n < flight(side)))
            def _():
                z_copy(side, sends(side) - 1 - n, target(side)).wait_send()
    for k in range(1, ns):
        for e in range(up_banks):
            u_copy(k, e, split).wait_send()

    @pl.when(jnp.logical_not(in_middle))
    def _():
        for e in range(banks):
            b_copy(e, blk % group).wait_send()

    for b in range(nb):
        @pl.when(b // per != split)
        def _():
            p_copy(b, split).wait_send()

            @pl.when(in_middle)
            def _():
                l_copy(b, split).wait_send()

    @pl.when(in_middle)
    def _():
        for k in range(1, nb):
            g_copy(k, upper).wait_send()

    for h in range(2):
        for k in range(1, nu):
            f_copy(k, h, sub).wait_send()


def shards(
    nb, ns, nu,
    attention_output_rows,
    residual,
    output_projection_weight,
    down_adapter_bank,
    up_adapter_bank,
    rollout_row_tenant,
    tenant_bank_entry,
    tenant_live_rank,
):
    rows, feats = attention_output_rows.shape
    own, cols = residual.shape
    banks, rank, _ = down_adapter_bank.shape
    up_banks = up_adapter_bank.shape[0]
    total = rollout_row_tenant.shape[0]
    wide = nb // 2 * banks * rank
    fc = PIECE
    per = own // rows
    pieces = feats // nu // fc
    items = (nb - 1) * pieces
    share = rows // nu
    dma = pltpu.SemaphoreType.DMA
    bf16 = jnp.bfloat16
    any_spec = pl.BlockSpec(memory_space=pltpu.HBM)
    vmem = pl.BlockSpec(memory_space=pltpu.VMEM)
    return pl.pallas_call(
        functools.partial(kernel, nb, ns, nu, fc),
        out_shape=pltpu.VMEM((own, cols), bf16),
        in_specs=[any_spec] * 8,
        out_specs=vmem,
        scratch_shapes=[
            pltpu.SMEM(tenant_bank_entry.shape, jnp.int32),
            pltpu.SMEM(tenant_live_rank.shape, jnp.int32),
            pltpu.VMEM((1, total), jnp.int32),
            pltpu.VMEM((rows, feats), bf16),
            pltpu.VMEM((nb, nu, pieces, rows, fc), bf16),
            pltpu.VMEM((feats, cols), bf16),
            pltpu.VMEM((own, cols), bf16),
            pltpu.VMEM((wide, feats), bf16),
            pltpu.VMEM((2 * wide, cols), bf16),
            pltpu.VMEM((total, wide), F32),
            pltpu.VMEM((nb, rows, cols), F32),
            pltpu.VMEM((nb, rows, cols), bf16),
            pltpu.VMEM((ns, per, rows, cols), bf16),
            pltpu.VMEM((per, share, wide), F32),
            pltpu.VMEM((nb, share, wide), F32),
            pltpu.VMEM((ns, per, share, wide), F32),
            pltpu.VMEM((2, nu, share, per * rank), bf16),
            pltpu.VMEM((own, 2 * wide), bf16),
            dma((2,)),
            dma((W_CHUNKS,)),
            dma((banks,)),
            pltpu.SemaphoreType.REGULAR,
            pltpu.SemaphoreType.REGULAR,
            dma((2, RING)),
            dma((items,)),
            dma((nu - 1, 2, 2)),
            dma((nu - 1, 2, 4)),
            dma((ns - 1, up_banks)),
            dma((ns - 1, up_banks)),
            dma((banks,)),
            dma((nb // 2, banks)),
            dma((nu - 1, nb // 2, banks)),
            dma((nu - 1, nb // 2, banks)),
            dma((nb,)),
            dma((ns - 1, per)),
            dma((nb,)),
            dma((ns - 1, per)),
            dma((nb - 1,)),
            dma((2,)),
            dma((nu - 1, 2)),
            dma((nu - 1, 2)),
        ],
        compiler_params=pltpu.CompilerParams(
            collective_id=0, has_side_effects=True, vmem_limit_bytes=60 * 2**20
        ),
    )(
        tenant_bank_entry,
        tenant_live_rank,
        attention_output_rows,
        residual,
        output_projection_weight,
        down_adapter_bank,
        up_adapter_bank,
        rollout_row_tenant.reshape(1, total),
    )


def solution(mesh):
    in_specs = (
        P(("groups", "blk"), "split"),
        P(("groups", "split"), ("blk", "sub")),
        P("split", ("blk", "sub")),
        P("blk", None, "split"),
        P("split", None, ("blk", "sub")),
        P("groups"),
        P(),
        P(),
    )
    out_specs = P(("groups", "split"), ("blk", "sub"))
    body = functools.partial(
        shards, mesh.shape["blk"], mesh.shape["split"], mesh.shape["sub"]
    )
    return jax.shard_map(body, mesh=mesh, in_specs=in_specs, out_specs=out_specs, check_vma=False)
```
